32 devices in a mesh: dp: 4 (over y, x), ctx: 8 (over z, core).
Axes of the slice: x: 2, y: 2, z: 4, core: 2. Of those that a mesh axis runs over, the one named last changes fastest.
Arguments:
- queries: bfloat16 [4096, 4096], P(('dp', 'ctx')), may hold values from -30 to 30
- key_input: bfloat16 [4096, 1024], P(('dp', 'ctx')), may hold values from -30 to 30
- value_input: bfloat16 [4096, 1024], P(('dp', 'ctx')), may hold values from -6 to 6
- out_grad: bfloat16 [4096, 4096], P(('dp', 'ctx')), may hold values from -6 to 6
- sink_logits: float32 [32], replicated, may hold values from 0 to 5
- doc_lengths: int32 [4, 4], replicated, may hold values from 1 to 4, 8 in all within a row
- assignment: int32 [4], replicated, may hold values from 0 to 3, each once
- stretch_map: int32 [16], replicated, may hold values from 0 to 15, each once
Outputs:
- attn_out: bfloat16 [4096, 4096], P(('dp', 'ctx'))
- query_grad: bfloat16 [4096, 4096], P(('dp', 'ctx'))
- key_grad: bfloat16 [4096, 1024], P(('dp', 'ctx'))
- value_grad: bfloat16 [4096, 1024], P(('dp', 'ctx'))
- sink_grad: float32 [32], replicated
The draws below stay inside these ranges and needn't reach their ends.
Inputs may be any that keep to these rules, and one draw needn't show every extreme that they name: `doc_lengths`: lengths count blocks of 128 tokens; every row sums to 8 and its longest document has exactly 4 blocks. `assignment`: A permutation of the sequences. `stretch_map`: A permutation of the stretches, the same for every sequence.
All inputs are finite; a program needn't handle non-finite values.
Results may differ from the reference program's by a relative error of at most 0.019.
Values may be sent and summed in bfloat16 or wider, within the bound.
No kernel may reach another device: no remote copies, remote signals or barrier semaphores. Data moves between devices by JAX's collectives and lax.ppermute only.
A program may use at most 128 MiB of HBM per device.

```python
import math
import jax
import jax.numpy as jnp
import numpy as np
from jax import lax

H = 32
KVH = 8
HD = 128
T_DEV = 128
BLOCK = 128
DOCS = 4
RATIO = 4
SEQ = 1024
SEQS = 4
TOKENS = 4096
STRETCH = 64
STRETCHES = 16
BLOCKS = 8
N_CTX = 8


def draw_queries(key, part):
    drawn = jax.random.truncated_normal(jax.random.fold_in(key, 11), -6.0, 6.0, (TOKENS, KVH, RATIO, HD), jnp.float32)
    return drawn.reshape(TOKENS, H * HD).astype(jnp.bfloat16)


def draw_key_input(key, part):
    drawn = jax.random.truncated_normal(jax.random.fold_in(key, 12), -6.0, 6.0, (TOKENS, KVH, HD), jnp.float32)
    return drawn.reshape(TOKENS, KVH * HD).astype(jnp.bfloat16)


def levels(own_key, dims, pieces, smallest, top_value):
    level = 1.0
    for axis_at, shards_of in pieces:
        draws = jax.random.uniform(jax.random.fold_in(jax.random.fold_in(own_key, 6), axis_at), (shards_of,), jnp.float32, smallest / len(pieces), top_value / len(pieces))
        level = level * jnp.repeat(jnp.exp(draws), dims[axis_at] // shards_of).reshape((-1,) + (1,) * (len(dims) - 1 - axis_at))
    return level


def length_profile(count, total, bound, skew):
    weights = [(1 << 20) // math.isqrt(rank ** skew) + 1 for rank in range(2, count + 1)]
    spare, holding = total - bound - (count - 1), [1] * (count - 1)
    while spare > 0:
        candidates = [i for i in range(count - 1) if holding[i] < bound]
        mass, left = sum([weights[i] for i in candidates]), spare
        for i in candidates:
            addition = min(bound - holding[i], max(1, left * weights[i] // mass), spare)
            holding[i] = holding[i] + addition
            spare = spare - addition
    return np.array([bound] + holding)


def uneven_parts(rng, amount, total, reach, lean):
    if amount == 2:
        one = jax.random.randint(rng, (), max(1, total - reach), min(reach, total - 1) + 1)
        return jnp.stack([one, total - one])
    sizes = jnp.asarray(length_profile(amount, total, reach, lean), jnp.int32)
    twos = (amount - 1) // 2
    source_of, receiver = sizes[1:1 + 2 * twos:2], sizes[2:2 + 2 * twos:2]
    room = jnp.minimum(source_of - 1, reach - receiver)
    moved = jax.random.randint(jax.random.fold_in(rng, 1), (twos,), 0, 1 << 20) % (room + 1)
    sizes = sizes.at[1:1 + 2 * twos:2].set(source_of - moved).at[2:2 + 2 * twos:2].set(receiver + moved)
    return sizes[jax.random.permutation(jax.random.fold_in(rng, 2), amount)]


def normal_values(own_key, extent, spread, reach, pieces=(), kind=jnp.bfloat16):
    loudness = levels(own_key, extent, pieces, -0.22, 0.18) if pieces else 1.0
    array = jax.random.normal(own_key, extent, jnp.float32) * spread * loudness
    return jnp.minimum(jnp.maximum(array, -reach), reach).astype(kind)


def setup_inputs(seed: int = 0) -> dict:
    arg_keys = jax.random.split(jax.random.key(seed), 9)
    queries = draw_queries(jax.random.fold_in(arg_keys[8], 71), 0)
    key_input = draw_key_input(jax.random.fold_in(arg_keys[8], 71), 0)
    value_input = normal_values(arg_keys[2], (TOKENS, KVH * HD), 1.0, 6.0, ((0, 32),))
    out_grad = normal_values(arg_keys[3], (TOKENS, H * HD), 1.0, 6.0, ((0, 32),))
    sink_logits = jnp.clip(jax.random.uniform(arg_keys[4], (H,), jnp.float32, 0.0, 5.0), 0.0, 5.0)
    doc_lengths = jax.vmap(lambda own: uneven_parts(own, DOCS, BLOCKS, BLOCKS // 2, 1))(jax.random.split(arg_keys[5], SEQS)).reshape((SEQS, DOCS)).astype(jnp.int32)
    assignment = jax.random.permutation(arg_keys[6], SEQS).astype(jnp.int32)
    stretch_map = jax.random.permutation(arg_keys[7], STRETCHES).astype(jnp.int32)
    return dict(queries=queries, key_input=key_input, value_input=value_input, out_grad=out_grad, sink_logits=sink_logits, doc_lengths=doc_lengths, assignment=assignment, stretch_map=stretch_map)


def true_positions(row_count, stretch_len, stretch_map):
    grid_shape = (row_count, stretch_map.shape[0])
    owners = lax.broadcasted_iota(jnp.int32, grid_shape, 0) // stretch_len
    picked = owners == lax.broadcasted_iota(jnp.int32, grid_shape, 1)
    leading = jnp.sum(jnp.where(picked, stretch_map[None, :], 0), axis=1).astype(jnp.int32)
    return (leading * stretch_len + jnp.arange(row_count, dtype=jnp.int32) % stretch_len).astype(jnp.int32)


def doc_numbers(positions, lengths):
    doc_ends = (jnp.cumsum(lengths) * BLOCK).astype(jnp.int32)
    return jnp.sum((positions[:, None] >= doc_ends[None, :]).astype(jnp.int32), axis=1).astype(jnp.int32)


def reference(queries, key_input, value_input, out_grad, sink_logits, doc_lengths, assignment, stretch_map):
    head_scale = HD ** -0.5
    positions = true_positions(SEQ, STRETCH, stretch_map)
    sink_heads = sink_logits.astype(jnp.float32).reshape(KVH, RATIO)

    def one_sequence(group_index):
        lengths = doc_lengths[assignment[group_index]]
        documents = doc_numbers(positions, lengths)
        first_row = (group_index * SEQ).astype(jnp.int32)
        query_seq = lax.dynamic_slice_in_dim(queries, first_row, SEQ, 0).reshape(SEQ, KVH, RATIO, HD)
        grad_seq = lax.dynamic_slice_in_dim(out_grad, first_row, SEQ, 0).reshape(SEQ, KVH, RATIO, HD)
        key_seq = lax.dynamic_slice_in_dim(key_input, first_row, SEQ, 0).reshape(SEQ, KVH, HD).astype(jnp.float32)
        value_seq = lax.dynamic_slice_in_dim(value_input, first_row, SEQ, 0).reshape(SEQ, KVH, HD).astype(jnp.float32)

        def one_block(running, block_index):
            key_sum, value_sum, sink_sum = running
            start_row = (block_index * T_DEV).astype(jnp.int32)
            query_block = lax.dynamic_slice_in_dim(query_seq, start_row, T_DEV, 0).astype(jnp.float32)
            grad_block = lax.dynamic_slice_in_dim(grad_seq, start_row, T_DEV, 0).astype(jnp.float32)
            query_pos = lax.dynamic_slice_in_dim(positions, start_row, T_DEV, 0)
            query_doc = lax.dynamic_slice_in_dim(documents, start_row, T_DEV, 0)
            allowed = ((query_doc[:, None] == documents[None, :]) & (positions[None, :] <= query_pos[:, None]))[:, None, None, :]
            scores = jnp.einsum('tgrd,ngd->tgrn', query_block, key_seq) * head_scale
            row_max = jnp.maximum(sink_heads[None], jnp.max(jnp.where(allowed, scores, -jnp.inf), axis=3))
            row_total = jnp.exp(sink_heads[None] - row_max) + jnp.sum(jnp.where(allowed, jnp.exp(scores - row_max[..., None]), 0.0), axis=3)
            weights = jnp.where(allowed, jnp.exp(scores - row_max[..., None]) / row_total[..., None], 0.0)
            weights_b = lax.optimization_barrier(weights.astype(jnp.bfloat16)).astype(jnp.float32)
            attn_heads = lax.optimization_barrier(jnp.einsum('tgrn,ngd->tgrd', weights_b, value_seq).astype(jnp.bfloat16))
            row_dot = jnp.sum(grad_block * attn_heads.astype(jnp.float32), axis=3)
            grad_weights = jnp.einsum('tgrd,ngd->tgrn', grad_block, value_seq)
            grad_scores = lax.optimization_barrier((weights * (grad_weights - row_dot[..., None]) * head_scale).astype(jnp.bfloat16)).astype(jnp.float32)
            query_block_grad = jnp.einsum('tgrn,ngd->tgrd', grad_scores, key_seq).astype(jnp.bfloat16)
            key_sum = key_sum + jnp.einsum('tgrn,tgrd->ngd', grad_scores, query_block)
            value_sum = value_sum + jnp.einsum('tgrn,tgrd->ngd', weights_b, grad_block)
            sink_sum = sink_sum - jnp.sum(jnp.exp(sink_heads[None] - row_max) / row_total * row_dot, axis=0)
            return (key_sum, value_sum, sink_sum), (attn_heads.reshape(T_DEV, H * HD), query_block_grad.reshape(T_DEV, H * HD))

        initial = (jnp.zeros((SEQ, KVH, HD), jnp.float32), jnp.zeros((SEQ, KVH, HD), jnp.float32), jnp.zeros((KVH, RATIO), jnp.float32))
        finals, stacked = lax.scan(one_block, initial, jnp.arange(N_CTX, dtype=jnp.int32))
        key_sum, value_sum, sink_sum = finals
        attn_seq = stacked[0].reshape(SEQ, H * HD)
        query_seq_grad = stacked[1].reshape(SEQ, H * HD)
        return (attn_seq, query_seq_grad, key_sum.reshape(SEQ, KVH * HD).astype(jnp.bfloat16), value_sum.reshape(SEQ, KVH * HD).astype(jnp.bfloat16), sink_sum)

    results = lax.map(one_sequence, jnp.arange(SEQS, dtype=jnp.int32))
    attn_out = results[0].reshape(TOKENS, H * HD)
    query_grad = results[1].reshape(TOKENS, H * HD)
    key_grad = results[2].reshape(TOKENS, KVH * HD)
    value_grad = results[3].reshape(TOKENS, KVH * HD)
    sink_grad = jnp.sum(results[4], axis=0).reshape(H)
    return (attn_out, query_grad, key_grad, value_grad, sink_grad)
```

```python
import functools
import math

import jax
import jax.numpy as jnp
from jax import lax
from jax.experimental import pallas as pl
from jax.experimental.pallas import tpu as pltpu
from jax.sharding import PartitionSpec as P

HD = 128
BLOCK = 128
STREAMS = 2
SCALE = HD**-0.5
LOG2E = math.log2(math.e)
MASKED = -1e30


def plan_kernel(stretch_len, place_ref, map_ref, lengths_ref, assign_ref, table_ref):
    chip, core, group = place_ref[0], place_ref[1], place_ref[2]
    stretches = map_ref.shape[0]
    sequences, documents = lengths_ref.shape
    chips = place_ref.shape[0] - 3
    per_chip = stretches // chips
    per_core = per_chip // 2
    limit = (table_ref.shape[1] - 1) // 2
    sequence = jnp.int32(0)
    for at in range(sequences):
        sequence = jnp.where(group == at, assign_ref[at], sequence)
    ends = []
    total = jnp.int32(0)
    for at in range(documents):
        total = total + lengths_ref[sequence, at] * (BLOCK // stretch_len)
        ends.append(total)

    def first_of_document(stretch):
        first = jnp.int32(0)
        for end in ends:
            first = jnp.where(stretch >= end, end, first)
        return first

    for row in range(per_chip):
        core_of_row = core if row < per_core else 1 - core
        slot = chip * per_chip + core_of_row * per_core + row % per_core
        mine = map_ref[slot]
        first = first_of_document(mine)

        def rows_of(key_slot):
            key_chip = key_slot // per_chip
            inner = key_slot - key_chip * per_chip
            key_core = inner // per_core
            inner = inner - key_core * per_core
            inner = inner + jnp.where(key_core == core, 0, per_core)
            ahead = key_chip - chip
            table = jnp.where(ahead > 0, chips - 1 + ahead, -ahead)
            partial = jnp.where(ahead < 0, ahead + chips, ahead)
            return (
                (table * per_chip + inner) * stretch_len,
                (partial * per_chip + inner) * stretch_len,
            )

        key_row, sum_row = rows_of(slot)
        for at in range(limit):
            table_ref[row, 1 + 2 * at] = key_row
            table_ref[row, 2 + 2 * at] = sum_row

        def visit(key_slot, count):
            other = map_ref[key_slot]
            seen = (other >= first) & (other < mine)

            @pl.when(seen)
            def _():
                key_row, sum_row = rows_of(key_slot)
                table_ref[row, 1 + 2 * count] = key_row
                table_ref[row, 2 + 2 * count] = sum_row

            return count + seen.astype(jnp.int32)

        table_ref[row, 0] = lax.fori_loop(0, stretches, visit, jnp.int32(1))


def attention_kernel(
    shape,
    place_ref,
    table_ref,
    sink_ref,
    q_ref,
    g_ref,
    pq_ref,
    pg_ref,
    *refs,
):
    heads, ratio, stretch_len, per_chip, chips, limit, stream = shape
    sources = refs[: 2 * chips - 1]
    o_ref, dq_ref, po_ref, pdq_ref = refs[2 * chips - 1 : 2 * chips + 3]
    partials = refs[2 * chips + 3 : 3 * chips + 3]
    sink_out = refs[3 * chips + 3]
    kv, dk_sum, dv_sum, sems = refs[3 * chips + 4 :]
    head = pl.program_id(0)
    rows = per_chip * stretch_len

    def copies(at):
        for index, source in enumerate(sources):
            for part in range(2):
                yield pltpu.make_async_copy(
                    source.at[:, pl.ds((part * heads + at) * HD, HD)],
                    kv.at[at, part, pl.ds(index * rows, rows)],
                    sems.at[at],
                )

    @pl.when(head == 0)
    def _():
        for at in range(heads):
            for copy in copies(at):
                copy.start()

    for at in range(heads):

        @pl.when(head == at)
        def _():
            for copy in copies(at):
                copy.wait()

    dk_sum[...] = jnp.zeros_like(dk_sum)
    dv_sum[...] = jnp.zeros_like(dv_sum)
    first_head = (place_ref[1] * STREAMS + stream) * heads * ratio + head * ratio
    sink = jnp.concatenate(
        [jnp.full((stretch_len, 1), sink_ref[first_head + at], jnp.float32) for at in range(ratio)],
        axis=0,
    ) * LOG2E
    block = ratio * stretch_len
    token = lax.broadcasted_iota(jnp.int32, (block, stretch_len), 0) % stretch_len
    causal = lax.broadcasted_iota(jnp.int32, (block, stretch_len), 1) <= token

    def take(ref, first):
        return jnp.concatenate(
            [ref[pl.ds(first, stretch_len), at * HD : (at + 1) * HD] for at in range(ratio)],
            axis=0,
        )

    def put(ref, first, value):
        for at in range(ratio):
            ref[pl.ds(first, stretch_len), at * HD : (at + 1) * HD] = value[
                at * stretch_len : (at + 1) * stretch_len
            ].astype(ref.dtype)

    def one_block(row, first, q_in, g_in, o_out, dq_out, slots):
        count = table_ref[row, 0]
        query, grad = take(q_in, first), take(g_in, first)
        key_rows = [pl.multiple_of(table_ref[row, 1 + 2 * at], stretch_len) for at in range(slots)]
        sum_rows = [pl.multiple_of(table_ref[row, 2 + 2 * at], stretch_len) for at in range(slots)]
        keys = jnp.concatenate([kv[head, 0, pl.ds(at, stretch_len)] for at in key_rows], axis=0)
        values = jnp.concatenate([kv[head, 1, pl.ds(at, stretch_len)] for at in key_rows], axis=0)
        dims = (((1,), (1,)), ((), ()))
        scores = lax.dot_general(query, keys, dims, preferred_element_type=jnp.float32)
        scores = scores * (SCALE * LOG2E)
        column = lax.broadcasted_iota(jnp.int32, scores.shape, 1)
        seen = column < count * stretch_len
        if slots * stretch_len == causal.shape[1]:
            seen = causal
        else:
            rest = slots * stretch_len - stretch_len
            token_all = lax.broadcasted_iota(jnp.int32, scores.shape, 0) % stretch_len
            seen = seen & ((column <= token_all) | (column >= stretch_len))
        scores = jnp.where(seen, scores, MASKED)
        row_max = jnp.maximum(sink, jnp.max(scores, axis=1, keepdims=True))
        terms = jnp.exp2(scores - row_max)
        sink_term = jnp.exp2(sink - row_max)
        total = sink_term + jnp.sum(terms, axis=1, keepdims=True)
        inverse = 1.0 / total
        weights = terms * inverse
        weights_b = weights.astype(jnp.bfloat16)
        attended = jnp.dot(weights_b, values, preferred_element_type=jnp.float32)
        attended = attended.astype(jnp.bfloat16)
        put(o_out, first, attended)
        row_dot = jnp.sum(
            grad.astype(jnp.float32) * attended.astype(jnp.float32), axis=1, keepdims=True
        )
        grad_weights = lax.dot_general(grad, values, dims, preferred_element_type=jnp.float32)
        grad_scores = (weights * ((grad_weights - row_dot) * SCALE)).astype(jnp.bfloat16)
        put(dq_out, first, jnp.dot(grad_scores, keys, preferred_element_type=jnp.float32))
        over_rows = (((0,), (0,)), ((), ()))
        dk = lax.dot_general(grad_scores, query, over_rows, preferred_element_type=jnp.float32)
        dv = lax.dot_general(weights_b, grad, over_rows, preferred_element_type=jnp.float32)
        for at, target in enumerate(sum_rows):
            part = slice(at * stretch_len, (at + 1) * stretch_len)
            dk_sum[pl.ds(target, stretch_len)] += dk[part]
            dv_sum[pl.ds(target, stretch_len)] += dv[part]
        terms_of_sink = (sink_term * inverse * row_dot).reshape(ratio, stretch_len, 1)
        return jnp.sum(terms_of_sink, axis=1)

    sink_out[0] = jnp.zeros_like(sink_out[0])
    half = per_chip // 2
    widths = []
    width = 2
    while width < limit:
        widths.append(width)
        width *= 2
    widths.append(limit)
    for ins, base in (((q_ref, g_ref, o_ref, dq_ref), 0), ((pq_ref, pg_ref, po_ref, pdq_ref), half)):

        def one_row(at, carry):
            row = base + at
            first = pl.multiple_of(at * stretch_len, stretch_len)
            count = table_ref[row, 0]
            below = 0
            for width in widths:

                @pl.when((count > below) & (count <= width))
                def _():
                    sink_out[0] -= jnp.broadcast_to(
                        one_block(row, first, *ins, width), sink_out.shape[1:]
                    )

                below = width
            return carry

        lax.fori_loop(0, half, one_row, 0)

    for at, partial in enumerate(partials):
        part = pl.ds(at * rows, rows)
        partial[:, :HD] = dk_sum[part].astype(partial.dtype)
        partial[:, HD:] = dv_sum[part].astype(partial.dtype)


def attend(stream, place, table, sinks, queries, out_grad, partner, sources, chips, limit, ratio):
    local_rows = queries.shape[0]
    heads = sources[0].shape[1] // (2 * HD)
    rows = sources[0].shape[0]
    per_chip = table.shape[0]
    stretch_len = rows // per_chip
    wide = ratio * HD
    shape = (heads, ratio, stretch_len, per_chip, chips, limit, stream)
    whole = STREAMS * heads
    here = pl.BlockSpec(
        (local_rows, wide), lambda g, place, table, sinks: (0, place[1] * whole + stream * heads + g)
    )
    there = pl.BlockSpec((local_rows, wide), lambda g, *_: (0, stream * heads + g))
    there_grad = pl.BlockSpec((local_rows, wide), lambda g, *_: (0, whole + stream * heads + g))
    out = pl.BlockSpec((local_rows, wide), lambda g, *_: (0, g))
    wide_out = jax.ShapeDtypeStruct((local_rows, heads * wide), jnp.bfloat16)
    partial = jax.ShapeDtypeStruct((rows, heads * 2 * HD), jnp.bfloat16)
    partial_spec = pl.BlockSpec((rows, 2 * HD), lambda g, *_: (0, g))
    return pl.pallas_call(
        functools.partial(attention_kernel, shape),
        grid_spec=pltpu.PrefetchScalarGridSpec(
            num_scalar_prefetch=3,
            grid=(heads,),
            in_specs=[here, here, there, there_grad]
            + [pl.BlockSpec(memory_space=pl.ANY)] * len(sources),
            out_specs=[out] * 4
            + [partial_spec] * chips
            + [pl.BlockSpec((1, ratio, HD), lambda g, *_: (g, 0, 0))],
            scratch_shapes=[
                pltpu.VMEM((heads, 2, len(sources) * rows, HD), jnp.bfloat16),
                pltpu.VMEM((chips * rows, HD), jnp.float32),
                pltpu.VMEM((chips * rows, HD), jnp.float32),
                pltpu.SemaphoreType.DMA((heads,)),
            ],
        ),
        out_shape=[wide_out] * 4
        + [partial] * chips
        + [jax.ShapeDtypeStruct((heads, ratio, HD), jnp.float32)],
        compiler_params=pltpu.CompilerParams(vmem_limit_bytes=40 << 20),
        cost_estimate=pl.CostEstimate(
            flops=6 * 2 * heads * rows * ratio * limit * stretch_len * HD,
            transcendentals=heads * rows * ratio * limit * stretch_len,
            bytes_accessed=4 << 20,
        ),
    )(place, table, sinks, queries, out_grad, partner, partner, *sources)


def send(value, pairs):
    return lax.ppermute(value, "ctx", pairs)


def along(chips, step, senders):
    return [
        (2 * chip + core, 2 * (chip + step) + core)
        for chip in senders
        if 0 <= chip + step < chips
        for core in range(2)
    ]


def gather_chain(value, chips):
    rightward, leftward = [value], [value]
    for hop in range(1, chips):
        rightward.append(send(rightward[-1], along(chips, 1, range(hop - 1, chips))))
        leftward.append(send(leftward[-1], along(chips, -1, range(0, chips - hop + 1))))
    return [value] + rightward[1:] + leftward[1:]


def add(left, right):
    return (left.astype(jnp.float32) + right.astype(jnp.float32)).astype(jnp.bfloat16)


def scatter_chain(partials, chips):
    rightward, leftward = partials[chips - 1], partials[1]
    for hop in range(1, chips):
        rightward = send(rightward, along(chips, 1, range(0, hop)))
        leftward = send(leftward, along(chips, -1, range(chips - hop, chips)))
        if hop < chips - 1:
            rightward = add(partials[chips - 1 - hop], rightward)
            leftward = add(partials[1 + hop], leftward)
    return (
        partials[0].astype(jnp.float32)
        + rightward.astype(jnp.float32)
        + leftward.astype(jnp.float32)
    ).astype(jnp.bfloat16)


def columns(table, first, count):
    return lax.dynamic_slice_in_dim(table, first, count, 1)


def per_device(
    queries, key_input, value_input, out_grad, sink_logits, doc_lengths, assignment, stretch_map
):
    local_rows = queries.shape[0]
    chips = lax.axis_size("ctx") // 2
    stretches = stretch_map.shape[0]
    stretch_len = local_rows * 2 * chips // stretches
    per_chip = stretches // chips
    head_count = sink_logits.shape[0]
    kv_heads = key_input.shape[1] // HD
    ratio = head_count // kv_heads
    limit = stretches // 2
    group = lax.axis_index("dp")
    index = lax.axis_index("ctx")
    chip, core = index // 2, index % 2
    swap = [(2 * at + side, 2 * at + 1 - side) for at in range(chips) for side in range(2)]
    half = kv_heads // 2 * HD
    width = half // STREAMS

    def key_values(side, stream):
        first = side * half + stream * width
        return jnp.concatenate(
            [columns(key_input, first, width), columns(value_input, first, width)], axis=1
        )

    sources = []
    for stream in range(STREAMS):
        received = send(key_values(1 - core, stream), swap)
        own = jnp.concatenate([key_values(core, stream), received], axis=0)
        sources.append(gather_chain(own, chips))
    partner = send(
        jnp.concatenate(
            [
                columns(queries, (1 - core) * half * ratio, half * ratio),
                columns(out_grad, (1 - core) * half * ratio, half * ratio),
            ],
            axis=1,
        ),
        swap,
    )
    place = jnp.concatenate(
        [jnp.stack([chip, core, group]).astype(jnp.int32), jnp.zeros((chips,), jnp.int32)]
    )
    smem = pl.BlockSpec(memory_space=pltpu.SMEM)
    table = pl.pallas_call(
        functools.partial(plan_kernel, stretch_len),
        in_specs=[smem] * 4,
        out_specs=smem,
        out_shape=jax.ShapeDtypeStruct((per_chip, 1 + 2 * limit), jnp.int32),
    )(place, stretch_map, doc_lengths, assignment)

    attended, query_grads, others, key_sums, sink_parts = [], [], [], [], []
    for stream in range(STREAMS):
        results = attend(
            stream, place, table, sink_logits, queries, out_grad, partner, sources[stream],
            chips, limit, ratio,
        )
        attended.append(results[0])
        query_grads.append(results[1])
        others += [results[2], results[3]]
        key_sums.append(scatter_chain(results[4 : 4 + chips], chips))
        sink_parts.append(results[4 + chips][:, :, 0].reshape(-1))

    sink_half = jnp.concatenate(sink_parts)
    blank = jnp.zeros_like(sink_half)
    sink_own = jnp.where(
        core == 0, jnp.concatenate([sink_half, blank]), jnp.concatenate([blank, sink_half])
    )
    sink_grad = lax.psum(sink_own, ("dp", "ctx"))

    def whole(mine, other):
        return jnp.where(
            core == 0, jnp.concatenate([mine, other], axis=1), jnp.concatenate([other, mine], axis=1)
        )

    back = send(jnp.concatenate(others, axis=1), swap)
    back = jnp.split(back, 2 * STREAMS, axis=1)
    attn_out = whole(jnp.concatenate(attended, axis=1), jnp.concatenate(back[0::2], axis=1))
    query_grad = whole(jnp.concatenate(query_grads, axis=1), jnp.concatenate(back[1::2], axis=1))

    sums = jnp.concatenate(
        [
            part[:, at : at + HD]
            for first in (0, HD)
            for part in key_sums
            for at in range(first, 2 * width, 2 * HD)
        ],
        axis=1,
    )
    mine, theirs = sums[:local_rows], send(sums[local_rows:], swap)
    key_grad = whole(mine[:, :half], theirs[:, :half])
    value_grad = whole(mine[:, half:], theirs[:, half:])
    return (attn_out, query_grad, key_grad, value_grad, sink_grad)


def solution(mesh):
    rows = P(("dp", "ctx"), None)
    return jax.shard_map(
        per_device,
        mesh=mesh,
        in_specs=(rows, rows, rows, rows, P(), P(), P(), P()),
        out_specs=(rows, rows, rows, rows, P()),
        check_vma=False,
    )
```

```python
import functools
import math

import jax
import jax.numpy as jnp
from jax import lax
from jax.experimental import pallas as pl
from jax.experimental.pallas import tpu as pltpu
from jax.sharding import PartitionSpec as P

HD = 128
BLOCK = 128
STREAMS = 2
SCALE = HD**-0.5
LOG2E = math.log2(math.e)
MASKED = -1e30


def plan_kernel(stretch_len, place_ref, map_ref, lengths_ref, assign_ref, table_ref):
    chip, core, group = place_ref[0], place_ref[1], place_ref[2]
    stretches = map_ref.shape[0]
    sequences, documents = lengths_ref.shape
    chips = place_ref.shape[0] - 3
    per_chip = stretches // chips
    per_core = per_chip // 2
    limit = (table_ref.shape[1] - 1) // 2
    sequence = jnp.int32(0)
    for at in range(sequences):
        sequence = jnp.where(group == at, assign_ref[at], sequence)
    ends = []
    total = jnp.int32(0)
    for at in range(documents):
        total = total + lengths_ref[sequence, at] * (BLOCK // stretch_len)
        ends.append(total)

    def first_of_document(stretch):
        first = jnp.int32(0)
        for end in ends:
            first = jnp.where(stretch >= end, end, first)
        return first

    for row in range(per_chip):
        core_of_row = core if row < per_core else 1 - core
        slot = chip * per_chip + core_of_row * per_core + row % per_core
        mine = map_ref[slot]
        first = first_of_document(mine)

        def rows_of(key_slot):
            key_chip = key_slot // per_chip
            inner = key_slot - key_chip * per_chip
            key_core = inner // per_core
            inner = inner - key_core * per_core
            inner = inner + jnp.where(key_core == core, 0, per_core)
            ahead = key_chip - chip
            table = jnp.where(ahead > 0, chips - 1 + ahead, -ahead)
            partial = jnp.where(ahead < 0, ahead + chips, ahead)
            return (
                (table * per_chip + inner) * stretch_len,
                (partial * per_chip + inner) * stretch_len,
            )

        key_row, sum_row = rows_of(slot)
        for at in range(limit):
            table_ref[row, 1 + 2 * at] = key_row
            table_ref[row, 2 + 2 * at] = sum_row

        def visit(key_slot, count):
            other = map_ref[key_slot]
            seen = (other >= first) & (other < mine)

            @pl.when(seen)
            def _():
                key_row, sum_row = rows_of(key_slot)
                table_ref[row, 1 + 2 * count] = key_row
                table_ref[row, 2 + 2 * count] = sum_row

            return count + seen.astype(jnp.int32)

        table_ref[row, 0] = lax.fori_loop(0, stretches, visit, jnp.int32(1))


def attention_kernel(shape, place_ref, table_ref, sink_ref, q_hbm, g_hbm, partner_hbm, *refs):
    heads, ratio, stretch_len, per_chip, chips, limit, stream = shape
    count_in = 2 * chips - 1
    sources, outs = refs[:count_in], refs[count_in : count_in + 2]
    partials = refs[count_in + 2 : count_in + 2 + chips]
    sink_out = refs[count_in + 2 + chips]
    kv, q_buf, g_buf, sums, sems = refs[count_in + 3 + chips :]
    chip, core = place_ref[0], place_ref[1]
    rows = per_chip * stretch_len
    local_rows = rows // 2
    wide = heads * ratio * HD
    here = pl.ds(pl.multiple_of((core * STREAMS + stream) * wide, HD), wide)
    loads = [
        (q_hbm.at[:, here], q_buf.at[pl.ds(0, local_rows)]),
        (g_hbm.at[:, here], g_buf.at[pl.ds(0, local_rows)]),
        (
            partner_hbm.at[:, pl.ds(stream * wide, wide)],
            q_buf.at[pl.ds(local_rows, local_rows)],
        ),
        (
            partner_hbm.at[:, pl.ds((STREAMS + stream) * wide, wide)],
            g_buf.at[pl.ds(local_rows, local_rows)],
        ),
    ]
    loads += [(source, kv.at[pl.ds(at * rows, rows)]) for at, source in enumerate(sources)]
    loads = [pltpu.make_async_copy(*pair, sems.at[at]) for at, pair in enumerate(loads)]
    for load in loads:
        load.start()
    sums[...] = jnp.zeros_like(sums)
    sink_out[...] = jnp.zeros_like(sink_out)
    block = ratio * stretch_len
    token = lax.broadcasted_iota(jnp.int32, (2 * stretch_len, block), 1) % stretch_len
    place = lax.broadcasted_iota(jnp.int32, (2 * stretch_len, block), 0)
    owner = lax.broadcasted_iota(jnp.int32, (1, block), 1) // stretch_len
    sinks = []
    for head in range(heads):
        first_head = ((core * STREAMS + stream) * heads + head) * ratio
        sink = jnp.zeros((1, block), jnp.float32)
        for at in range(ratio):
            sink = jnp.where(owner == at, sink_ref[first_head + at] * LOG2E, sink)
        sinks.append(sink)
    for load in loads:
        load.wait()

    def take(ref, first, head):
        first_lane = head * ratio * HD
        return jnp.concatenate(
            [
                ref[pl.ds(first, stretch_len), first_lane + at * HD : first_lane + (at + 1) * HD]
                for at in range(ratio)
            ],
            axis=0,
        )

    def put(ref, first, head, value):
        first_lane = head * ratio * HD
        for at in range(ratio):
            ref[pl.ds(first, stretch_len), first_lane + at * HD : first_lane + (at + 1) * HD] = (
                value[at * stretch_len : (at + 1) * stretch_len].astype(ref.dtype)
            )

    def one_block(row, slots):
        count = table_ref[row, 0]
        first = pl.multiple_of(row * stretch_len, stretch_len)
        key_rows = [pl.multiple_of(table_ref[row, 1 + 2 * at], stretch_len) for at in range(slots)]
        sum_rows = [pl.multiple_of(table_ref[row, 2 + 2 * at], stretch_len) for at in range(slots)]
        order = list(range(1, slots - 1)) + [slots - 1, 0]
        empty = jnp.where(count == slots, 0, 4 * stretch_len)
        seen = jnp.where(place < stretch_len, empty, place - stretch_len) <= token
        across = (((1,), (1,)), ((), ()))
        down = (((0,), (0,)), ((), ()))
        for head in range(heads):
            query, grad = take(q_buf, first, head), take(g_buf, first, head)
            keys = jnp.concatenate(
                [kv[pl.ds(key_rows[at], stretch_len), head * HD : (head + 1) * HD] for at in order],
                axis=0,
            )
            values = jnp.concatenate(
                [
                    kv[
                        pl.ds(key_rows[at], stretch_len),
                        (heads + head) * HD : (heads + head + 1) * HD,
                    ]
                    for at in order
                ],
                axis=0,
            )
            scores = lax.dot_general(keys, query, across, preferred_element_type=jnp.float32)
            grad_weights = lax.dot_general(values, grad, across, preferred_element_type=jnp.float32)
            edge = jnp.where(seen, scores[(slots - 2) * stretch_len :], MASKED)
            if slots > 2:
                scores = jnp.concatenate([scores[: (slots - 2) * stretch_len], edge], axis=0)
            else:
                scores = edge
            scores = scores * (SCALE * LOG2E)
            row_max = jnp.maximum(sinks[head], jnp.max(scores, axis=0, keepdims=True))
            terms = jnp.exp2(scores - row_max)
            sink_term = jnp.exp2(sinks[head] - row_max)
            inverse = 1.0 / (sink_term + jnp.sum(terms, axis=0, keepdims=True))
            weights = terms * inverse
            weights_b = weights.astype(jnp.bfloat16)
            row_dot = jnp.sum(weights * grad_weights, axis=0, keepdims=True)
            grad_scores = (weights * (grad_weights - row_dot)).astype(jnp.bfloat16)
            dv = jnp.dot(weights_b, grad, preferred_element_type=jnp.float32)
            dk = jnp.dot(grad_scores, query, preferred_element_type=jnp.float32)
            attended = lax.dot_general(weights_b, values, down, preferred_element_type=jnp.float32)
            dq = lax.dot_general(grad_scores, keys, down, preferred_element_type=jnp.float32) * SCALE
            put(outs[0], first, head, attended)
            put(outs[1], first, head, dq)
            for spot, at in enumerate(order):
                part = slice(spot * stretch_len, (spot + 1) * stretch_len)
                target = pl.ds(sum_rows[at], stretch_len)
                sums[target, 2 * head * HD : (2 * head + 1) * HD] += dk[part]
                sums[target, (2 * head + 1) * HD : (2 * head + 2) * HD] += dv[part]
            sink_out[head] -= sink_term * inverse * row_dot

    widths = []
    width = 2
    while width < limit:
        widths.append(width)
        width += 2
    widths.append(limit)

    def one_row(row, carry):
        count = table_ref[row, 0]
        below = 0
        for width in widths:

            @pl.when((count > below) & (count <= width))
            def _():
                one_block(row, width)

            below = width
        return carry

    lax.fori_loop(0, per_chip, one_row, 0)
    for at, partial in enumerate(partials):
        for head in range(heads):
            left = slice(2 * head * HD, (2 * head + 1) * HD)
            partial[:, left] = (sums[at * rows : (at + 1) * rows, left] * SCALE).astype(partial.dtype)
            right = slice((2 * head + 1) * HD, (2 * head + 2) * HD)
            partial[:, right] = sums[at * rows : (at + 1) * rows, right].astype(partial.dtype)


def attend(stream, place, table, sinks, queries, out_grad, partner, sources, chips, limit, ratio):
    heads = sources[0].shape[1] // (2 * HD)
    rows = sources[0].shape[0]
    per_chip = table.shape[0]
    stretch_len = rows // per_chip
    wide = heads * ratio * HD
    shape = (heads, ratio, stretch_len, per_chip, chips, limit, stream)
    smem, hbm = pl.BlockSpec(memory_space=pltpu.SMEM), pl.BlockSpec(memory_space=pl.ANY)
    vmem = pl.BlockSpec(memory_space=pltpu.VMEM)
    return pl.pallas_call(
        functools.partial(attention_kernel, shape),
        in_specs=[smem] * 3 + [hbm] * (3 + len(sources)),
        out_specs=[vmem] * (3 + chips),
        scratch_shapes=[
            pltpu.VMEM((len(sources) * rows, heads * 2 * HD), jnp.bfloat16),
            pltpu.VMEM((rows, wide), jnp.bfloat16),
            pltpu.VMEM((rows, wide), jnp.bfloat16),
            pltpu.VMEM((chips * rows, heads * 2 * HD), jnp.float32),
            pltpu.SemaphoreType.DMA((4 + len(sources),)),
        ],
        out_shape=[jax.ShapeDtypeStruct((rows, wide), jnp.bfloat16)] * 2
        + [jax.ShapeDtypeStruct((rows, heads * 2 * HD), jnp.bfloat16)] * chips
        + [jax.ShapeDtypeStruct((heads, 1, ratio * stretch_len), jnp.float32)],
        compiler_params=pltpu.CompilerParams(vmem_limit_bytes=16 << 20),
        cost_estimate=pl.CostEstimate(
            flops=6 * 2 * heads * rows * ratio * limit * stretch_len * HD,
            transcendentals=heads * rows * ratio * limit * stretch_len,
            bytes_accessed=4 << 20,
        ),
    )(place, table, sinks, queries, out_grad, partner, *sources)


def send(value, pairs):
    return lax.ppermute(value, "ctx", pairs)


def along(chips, step, senders):
    return [
        (2 * chip + core, 2 * (chip + step) + core)
        for chip in senders
        if 0 <= chip + step < chips
        for core in range(2)
    ]


def gather_hop(rightward, leftward, hop, chips):
    return (
        send(rightward, along(chips, 1, range(hop - 1, chips))),
        send(leftward, along(chips, -1, range(0, chips - hop + 1))),
    )


def scatter_hop(rightward, leftward, hop, chips):
    return (
        send(rightward, along(chips, 1, range(0, hop))),
        send(leftward, along(chips, -1, range(chips - hop, chips))),
    )


def after(values, *earlier):
    return lax.optimization_barrier((tuple(values), earlier))[0]


def add(left, right):
    return (left.astype(jnp.float32) + right.astype(jnp.float32)).astype(jnp.bfloat16)


def add3(first, second, third):
    total = first.astype(jnp.float32) + second.astype(jnp.float32) + third.astype(jnp.float32)
    return total.astype(jnp.bfloat16)


def columns(table, first, count):
    return lax.dynamic_slice_in_dim(table, first, count, 1)


def per_device(
    queries, key_input, value_input, out_grad, sink_logits, doc_lengths, assignment, stretch_map
):
    local_rows = queries.shape[0]
    chips = lax.axis_size("ctx") // 2
    stretches = stretch_map.shape[0]
    stretch_len = local_rows * 2 * chips // stretches
    per_chip = stretches // chips
    head_count = sink_logits.shape[0]
    kv_heads = key_input.shape[1] // HD
    ratio = head_count // kv_heads
    limit = stretches // 2
    group = lax.axis_index("dp")
    index = lax.axis_index("ctx")
    chip, core = index // 2, index % 2
    swap = [(2 * at + side, 2 * at + 1 - side) for at in range(chips) for side in range(2)]
    half = kv_heads // 2 * HD
    width = half // STREAMS

    def key_values(side, stream):
        first = side * half + stream * width
        return jnp.concatenate(
            [columns(key_input, first, width), columns(value_input, first, width)], axis=1
        )

    received = send(
        jnp.concatenate([key_values(1 - core, stream) for stream in range(STREAMS)], axis=1), swap
    )
    own = [
        jnp.concatenate(
            [key_values(core, at), received[:, 2 * width * at : 2 * width * (at + 1)]], axis=0
        )
        for at in range(STREAMS)
    ]
    partner = send(
        jnp.concatenate(
            [
                columns(queries, (1 - core) * half * ratio, half * ratio),
                columns(out_grad, (1 - core) * half * ratio, half * ratio),
            ],
            axis=1,
        ),
        swap,
    )
    place = jnp.concatenate(
        [jnp.stack([chip, core, group]).astype(jnp.int32), jnp.zeros((chips,), jnp.int32)]
    )
    smem = pl.BlockSpec(memory_space=pltpu.SMEM)
    table = pl.pallas_call(
        functools.partial(plan_kernel, stretch_len),
        in_specs=[smem] * 4,
        out_specs=smem,
        out_shape=jax.ShapeDtypeStruct((per_chip, 1 + 2 * limit), jnp.int32),
    )(place, stretch_map, doc_lengths, assignment)

    def compute(stream, right, left):
        results = attend(
            stream, place, table, sink_logits, queries, out_grad, partner,
            [own[stream]] + right + left, chips, limit, ratio,
        )
        heads = results[-1].shape[0]
        sinks = jnp.sum(results[-1].reshape(heads, ratio, -1), axis=2).reshape(-1)
        others = jnp.concatenate([part[local_rows:] for part in results[:2]], axis=1)
        return results[:2], results[2:-1], sinks, others

    def gathered(stream, right, left, hop):
        rightward, leftward = (right[-1], left[-1]) if right else (own[stream], own[stream])
        rightward, leftward = gather_hop(rightward, leftward, hop, chips)
        right.append(rightward)
        left.append(leftward)

    def scattered(partials, running, hop):
        if running is None:
            return scatter_hop(partials[chips - 1], partials[1], hop, chips)
        return scatter_hop(
            add(partials[chips - hop], running[0]), add(partials[hop], running[1]), hop, chips
        )

    def finished(partials, running):
        total = add3(partials[0], *running)
        return total[:local_rows], send(total[local_rows:], swap)

    first_right, first_left, second_right, second_left = [], [], [], []
    for hop in range(1, chips):
        if hop == chips - 1:
            if first_right:
                (own[1],) = after([own[1]], first_right[-1], first_left[-1])
            gathered(1, second_right, second_left, 1)
        gathered(0, first_right, first_left, hop)
    first_out, first_sums, first_sink, first_others = compute(0, first_right, first_left)
    second_right[0], second_left[0] = after([second_right[0], second_left[0]], first_sink)
    running = None
    for hop in range(2, chips):
        gathered(1, second_right, second_left, hop)
        running = scattered(first_sums, running, hop - 1)
    first_back = send(first_others, swap)
    second_out, second_sums, second_sink, second_others = compute(1, second_right, second_left)
    if running is not None:
        running = after(running, second_sink)
    running = scattered(first_sums, running, chips - 1)

    blank = jnp.zeros_like(first_sink)
    sink_grad = jnp.concatenate([first_sink, second_sink])
    sink_grad = jnp.where(
        core == 0,
        jnp.concatenate([sink_grad, blank, blank]),
        jnp.concatenate([blank, blank, sink_grad]),
    )
    sink_grad = jnp.pad(sink_grad.reshape(1, -1), ((0, 7), (0, 128 - head_count)))
    steps = [("dp", 1 << at) for at in range((lax.axis_size("dp") - 1).bit_length())]
    steps += [("ctx", 1 << at) for at in range((2 * chips - 1).bit_length())]

    def exchange(value, step):
        name, bit = step
        size = lax.axis_size(name)
        return value + lax.ppermute(value, name, [(at, at ^ bit) for at in range(size)])

    tail = None
    per_hop = -(-len(steps) // (chips - 1))
    for hop in range(1, chips):
        tail = scattered(second_sums, tail, hop)
        if hop == 1:
            first_total = finished(first_sums, running)
        for step in steps[:per_hop]:
            sink_grad = exchange(sink_grad, step)
        steps = steps[per_hop:]
        if hop < chips - 1:
            tail = after(tail, sink_grad)
    second_back = send(second_others, swap)
    second_total = finished(second_sums, tail)
    sink_grad = sink_grad[0, :head_count]

    def whole(mine, other):
        return jnp.where(
            core == 0, jnp.concatenate(mine + other, axis=1), jnp.concatenate(other + mine, axis=1)
        )

    wide = width * ratio
    attn_out, query_grad = [
        whole(
            [part[at][:local_rows] for part in (first_out, second_out)],
            [part[:, at * wide : (at + 1) * wide] for part in (first_back, second_back)],
        )
        for at in range(2)
    ]
    key_grad, value_grad = [
        whole(
            *[
                [
                    part[side][:, at : at + HD]
                    for part in (first_total, second_total)
                    for at in range(first, 2 * width, 2 * HD)
                ]
                for side in range(2)
            ]
        )
        for first in (0, HD)
    ]
    return (attn_out, query_grad, key_grad, value_grad, sink_grad)


def solution(mesh):
    rows = P(("dp", "ctx"), None)
    return jax.shard_map(
        per_device,
        mesh=mesh,
        in_specs=(rows, rows, rows, rows, P(), P(), P(), P()),
        out_specs=(rows, rows, rows, rows, P()),
        check_vma=False,
    )
```

```python
import functools
import math

import jax
import jax.numpy as jnp
from jax import lax
from jax.experimental import pallas as pl
from jax.experimental.pallas import tpu as pltpu
from jax.sharding import PartitionSpec as P

HD = 128
BLOCK = 128
STREAMS = 2
SCALE = HD**-0.5
LOG2E = math.log2(math.e)
MASKED = -1e30


def fill_table(
    chip, core, group, chips, stretch_len, map_ref, lengths_ref, assign_ref, table_ref
):
    stretches = map_ref.shape[0]
    sequences, documents = lengths_ref.shape
    per_chip = stretches // chips
    per_core = per_chip // 2
    limit = (table_ref.shape[1] - 1) // 2
    sequence = jnp.int32(0)
    for at in range(sequences):
        sequence = jnp.where(group == at, assign_ref[at], sequence)
    ends = []
    total = jnp.int32(0)
    for at in range(documents):
        total = total + lengths_ref[sequence, at] * (BLOCK // stretch_len)
        ends.append(total)

    def first_of_document(stretch):
        first = jnp.int32(0)
        for end in ends:
            first = jnp.where(stretch >= end, end, first)
        return first

    for row in range(per_chip):
        core_of_row = core if row < per_core else 1 - core
        slot = chip * per_chip + core_of_row * per_core + row % per_core
        mine = map_ref[slot]
        first = first_of_document(mine)

        def rows_of(key_slot):
            key_chip = key_slot // per_chip
            inner = key_slot - key_chip * per_chip
            key_core = inner // per_core
            inner = inner - key_core * per_core
            inner = inner + jnp.where(key_core == core, 0, per_core)
            ahead = key_chip - chip
            table = jnp.where(ahead > 0, chips - 1 + ahead, -ahead)
            partial = jnp.where(ahead < 0, ahead + chips, ahead)
            return (
                (table * per_chip + inner) * stretch_len,
                (partial * per_chip + inner) * stretch_len,
            )

        key_row, sum_row = rows_of(slot)
        for at in range(limit):
            table_ref[row, 1 + 2 * at] = key_row
            table_ref[row, 2 + 2 * at] = sum_row

        def visit(key_slot, count):
            other = map_ref[key_slot]
            seen = (other >= first) & (other < mine)

            @pl.when(seen)
            def _():
                key_row, sum_row = rows_of(key_slot)
                table_ref[row, 1 + 2 * count] = key_row
                table_ref[row, 2 + 2 * count] = sum_row

            return count + seen.astype(jnp.int32)

        table_ref[row, 0] = lax.fori_loop(0, stretches, visit, jnp.int32(1))


def attention_kernel(
    shape, map_ref, lengths_ref, assign_ref, sink_ref, q_hbm, g_hbm, partner_hbm, *refs
):
    heads, ratio, stretch_len, per_chip, chips, limit, stream = shape
    count_in = 2 * chips - 1
    sources, outs = refs[:count_in], refs[count_in : count_in + 2]
    partials = refs[count_in + 2 : count_in + 2 + chips]
    sink_out = refs[count_in + 2 + chips]
    kv, q_buf, g_buf, sums, table_ref, sems = refs[count_in + 3 + chips :]
    index = lax.axis_index("ctx")
    chip, core = index // 2, index % 2
    rows = per_chip * stretch_len
    local_rows = rows // 2
    wide = heads * ratio * HD
    here = pl.ds(pl.multiple_of((core * STREAMS + stream) * wide, HD), wide)
    loads = [
        (q_hbm.at[:, here], q_buf.at[pl.ds(0, local_rows)]),
        (g_hbm.at[:, here], g_buf.at[pl.ds(0, local_rows)]),
        (
            partner_hbm.at[:, pl.ds(stream * wide, wide)],
            q_buf.at[pl.ds(local_rows, local_rows)],
        ),
        (
            partner_hbm.at[:, pl.ds((STREAMS + stream) * wide, wide)],
            g_buf.at[pl.ds(local_rows, local_rows)],
        ),
    ]
    loads += [(source, kv.at[pl.ds(at * rows, rows)]) for at, source in enumerate(sources)]
    loads = [pltpu.make_async_copy(*pair, sems.at[at]) for at, pair in enumerate(loads)]
    for load in loads:
        load.start()
    fill_table(
        chip,
        core,
        lax.axis_index("dp"),
        chips,
        stretch_len,
        map_ref,
        lengths_ref,
        assign_ref,
        table_ref,
    )
    sums[...] = jnp.zeros_like(sums)
    sink_out[...] = jnp.zeros_like(sink_out)
    block = ratio * stretch_len
    token = lax.broadcasted_iota(jnp.int32, (2 * stretch_len, block), 1) % stretch_len
    place = lax.broadcasted_iota(jnp.int32, (2 * stretch_len, block), 0)
    owner = lax.broadcasted_iota(jnp.int32, (1, block), 1) // stretch_len
    sinks = []
    for head in range(heads):
        first_head = ((core * STREAMS + stream) * heads + head) * ratio
        sink = jnp.zeros((1, block), jnp.float32)
        for at in range(ratio):
            sink = jnp.where(owner == at, sink_ref[first_head + at] * LOG2E, sink)
        sinks.append(sink)
    for load in loads:
        load.wait()

    def take(ref, first, head):
        first_lane = head * ratio * HD
        return jnp.concatenate(
            [
                ref[pl.ds(first, stretch_len), first_lane + at * HD : first_lane + (at + 1) * HD]
                for at in range(ratio)
            ],
            axis=0,
        )

    def put(ref, first, head, value):
        first_lane = head * ratio * HD
        for at in range(ratio):
            ref[pl.ds(first, stretch_len), first_lane + at * HD : first_lane + (at + 1) * HD] = (
                value[at * stretch_len : (at + 1) * stretch_len].astype(ref.dtype)
            )

    def one_block(row, slots):
        count = table_ref[row, 0]
        first = pl.multiple_of(row * stretch_len, stretch_len)
        key_rows = [pl.multiple_of(table_ref[row, 1 + 2 * at], stretch_len) for at in range(slots)]
        sum_rows = [pl.multiple_of(table_ref[row, 2 + 2 * at], stretch_len) for at in range(slots)]
        order = list(range(1, slots - 1)) + [slots - 1, 0]
        empty = jnp.where(count == slots, 0, 4 * stretch_len)
        seen = jnp.where(place < stretch_len, empty, place - stretch_len) <= token
        across = (((1,), (1,)), ((), ()))
        down = (((0,), (0,)), ((), ()))
        for head in range(heads):
            query, grad = take(q_buf, first, head), take(g_buf, first, head)
            keys = jnp.concatenate(
                [kv[pl.ds(key_rows[at], stretch_len), head * HD : (head + 1) * HD] for at in order],
                axis=0,
            )
            values = jnp.concatenate(
                [
                    kv[
                        pl.ds(key_rows[at], stretch_len),
                        (heads + head) * HD : (heads + head + 1) * HD,
                    ]
                    for at in order
                ],
                axis=0,
            )
            scores = lax.dot_general(keys, query, across, preferred_element_type=jnp.float32)
            grad_weights = lax.dot_general(values, grad, across, preferred_element_type=jnp.float32)
            edge = jnp.where(seen, scores[(slots - 2) * stretch_len :], MASKED)
            if slots > 2:
                scores = jnp.concatenate([scores[: (slots - 2) * stretch_len], edge], axis=0)
            else:
                scores = edge
            scores = scores * (SCALE * LOG2E)
            row_max = jnp.maximum(sinks[head], jnp.max(scores, axis=0, keepdims=True))
            terms = jnp.exp2(scores - row_max)
            sink_term = jnp.exp2(sinks[head] - row_max)
            inverse = 1.0 / (sink_term + jnp.sum(terms, axis=0, keepdims=True))
            weights = terms * inverse
            weights_b = weights.astype(jnp.bfloat16)
            row_dot = jnp.sum(weights * grad_weights, axis=0, keepdims=True)
            grad_scores = (weights * (grad_weights - row_dot)).astype(jnp.bfloat16)
            dv = jnp.dot(weights_b, grad, preferred_element_type=jnp.float32)
            dk = jnp.dot(grad_scores, query, preferred_element_type=jnp.float32)
            attended = lax.dot_general(weights_b, values, down, preferred_element_type=jnp.float32)
            dq = lax.dot_general(grad_scores, keys, down, preferred_element_type=jnp.float32) * SCALE
            put(outs[0], first, head, attended)
            put(outs[1], first, head, dq)
            for spot, at in enumerate(order):
                part = slice(spot * stretch_len, (spot + 1) * stretch_len)
                target = pl.ds(sum_rows[at], stretch_len)
                sums[target, head * HD : (head + 1) * HD] += dk[part]
                sums[target, (heads + head) * HD : (heads + head + 1) * HD] += dv[part]
            sink_out[head] -= sink_term * inverse * row_dot

    widths = []
    width = 2
    while width < limit:
        widths.append(width)
        width += 2
    widths.append(limit)

    def one_row(row, carry):
        count = table_ref[row, 0]
        below = 0
        for width in widths:

            @pl.when((count > below) & (count <= width))
            def _():
                one_block(row, width)

            below = width
        return carry

    lax.fori_loop(0, per_chip, one_row, 0)
    for at, partial in enumerate(partials):
        part = slice(at * rows, (at + 1) * rows)
        partial[:, : heads * HD] = (sums[part, : heads * HD] * SCALE).astype(partial.dtype)
        partial[:, heads * HD :] = sums[part, heads * HD :].astype(partial.dtype)


def attend(stream, layout, sinks, queries, out_grad, partner, sources, chips, limit, ratio):
    heads = sources[0].shape[1] // (2 * HD)
    rows = sources[0].shape[0]
    per_chip = layout[0].shape[0] // chips
    stretch_len = rows // per_chip
    wide = heads * ratio * HD
    shape = (heads, ratio, stretch_len, per_chip, chips, limit, stream)
    smem, hbm = pl.BlockSpec(memory_space=pltpu.SMEM), pl.BlockSpec(memory_space=pltpu.HBM)
    vmem = pl.BlockSpec(memory_space=pltpu.VMEM)
    return pl.pallas_call(
        functools.partial(attention_kernel, shape),
        in_specs=[smem] * 4 + [hbm] * (3 + len(sources)),
        out_specs=[vmem] * (3 + chips),
        scratch_shapes=[
            pltpu.VMEM((len(sources) * rows, heads * 2 * HD), jnp.bfloat16),
            pltpu.VMEM((rows, wide), jnp.bfloat16),
            pltpu.VMEM((rows, wide), jnp.bfloat16),
            pltpu.VMEM((chips * rows, heads * 2 * HD), jnp.float32),
            pltpu.SMEM((per_chip, 1 + 2 * limit), jnp.int32),
            pltpu.SemaphoreType.DMA((4 + len(sources),)),
        ],
        out_shape=[jax.ShapeDtypeStruct((rows, wide), jnp.bfloat16)] * 2
        + [jax.ShapeDtypeStruct((rows, heads * 2 * HD), jnp.bfloat16)] * chips
        + [jax.ShapeDtypeStruct((heads, 1, ratio * stretch_len), jnp.float32)],
        compiler_params=pltpu.CompilerParams(vmem_limit_bytes=60 << 20),
        cost_estimate=pl.CostEstimate(
            flops=6 * 2 * heads * rows * ratio * limit * stretch_len * HD,
            transcendentals=heads * rows * ratio * limit * stretch_len,
            bytes_accessed=4 << 20,
        ),
    )(*layout, sinks, queries, out_grad, partner, *sources)


def send(value, pairs):
    return lax.ppermute(value, "ctx", pairs)


def along(chips, step, senders):
    return [
        (2 * chip + core, 2 * (chip + step) + core)
        for chip in senders
        if 0 <= chip + step < chips
        for core in range(2)
    ]


def gather_hop(rightward, leftward, hop, chips):
    return (
        send(rightward, along(chips, 1, range(hop - 1, chips))),
        send(leftward, along(chips, -1, range(0, chips - hop + 1))),
    )


def scatter_hop(rightward, leftward, hop, chips):
    return (
        send(rightward, along(chips, 1, range(0, hop))),
        send(leftward, along(chips, -1, range(chips - hop, chips))),
    )


def add(left, right):
    return (left.astype(jnp.float32) + right.astype(jnp.float32)).astype(jnp.bfloat16)


def add3(first, second, third):
    total = first.astype(jnp.float32) + second.astype(jnp.float32) + third.astype(jnp.float32)
    return total.astype(jnp.bfloat16)


def columns(table, first, count):
    return lax.dynamic_slice_in_dim(table, first, count, 1)


def per_device(
    queries, key_input, value_input, out_grad, sink_logits, doc_lengths, assignment, stretch_map
):
    local_rows = queries.shape[0]
    chips = lax.axis_size("ctx") // 2
    stretches = stretch_map.shape[0]
    stretch_len = local_rows * 2 * chips // stretches
    per_chip = stretches // chips
    head_count = sink_logits.shape[0]
    kv_heads = key_input.shape[1] // HD
    ratio = head_count // kv_heads
    limit = stretches // 2
    group = lax.axis_index("dp")
    index = lax.axis_index("ctx")
    chip, core = index // 2, index % 2
    swap = [(2 * at + side, 2 * at + 1 - side) for at in range(chips) for side in range(2)]
    half = kv_heads // 2 * HD
    width = half // STREAMS

    def key_values(side, stream):
        first = side * half + stream * width
        return jnp.concatenate(
            [columns(key_input, first, width), columns(value_input, first, width)], axis=1
        )

    received = send(
        jnp.concatenate([key_values(1 - core, stream) for stream in range(STREAMS)], axis=1), swap
    )
    own = [
        jnp.concatenate(
            [key_values(core, at), received[:, 2 * width * at : 2 * width * (at + 1)]], axis=0
        )
        for at in range(STREAMS)
    ]
    partner = send(
        jnp.concatenate(
            [
                columns(queries, (1 - core) * half * ratio, half * ratio),
                columns(out_grad, (1 - core) * half * ratio, half * ratio),
            ],
            axis=1,
        ),
        swap,
    )
    layout = (stretch_map, doc_lengths, assignment)

    def compute(stream, right, left):
        results = attend(
            stream, layout, sink_logits, queries, out_grad, partner,
            [own[stream]] + right + left, chips, limit, ratio,
        )
        heads = results[-1].shape[0]
        sinks = jnp.sum(results[-1].reshape(heads, ratio, -1), axis=2).reshape(-1)
        others = jnp.concatenate([part[local_rows:] for part in results[:2]], axis=1)
        return results[:2], results[2:-1], sinks, others

    def gathered(stream, right, left, hop):
        rightward, leftward = (right[-1], left[-1]) if right else (own[stream], own[stream])
        rightward, leftward = gather_hop(rightward, leftward, hop, chips)
        right.append(rightward)
        left.append(leftward)

    def scattered(partials, running, hop):
        if running is None:
            return scatter_hop(partials[chips - 1], partials[1], hop, chips)
        return scatter_hop(
            add(partials[chips - hop], running[0]), add(partials[hop], running[1]), hop, chips
        )

    def finished(partials, running):
        total = add3(partials[0], *running)
        return total[:local_rows], send(total[local_rows:], swap)

    first_right, first_left, second_right, second_left = [], [], [], []
    for hop in range(1, chips):
        gathered(0, first_right, first_left, hop)
        gathered(1, second_right, second_left, hop)
    first_out, first_sums, first_sink, first_others = compute(0, first_right, first_left)
    first_run = scattered(first_sums, None, 1)
    second_out, second_sums, second_sink, second_others = compute(1, second_right, second_left)
    second_run = scattered(second_sums, None, 1)

    blank = jnp.zeros_like(first_sink)
    sink_grad = jnp.concatenate([first_sink, second_sink])
    sink_grad = jnp.where(
        core == 0,
        jnp.concatenate([sink_grad, blank, blank]),
        jnp.concatenate([blank, blank, sink_grad]),
    )
    sink_grad = jnp.pad(sink_grad.reshape(1, -1), ((0, 7), (0, 128 - head_count)))
    steps = [("dp", 1 << at) for at in range((lax.axis_size("dp") - 1).bit_length())]
    steps += [("ctx", 1 << at) for at in range((2 * chips - 1).bit_length())]

    def exchange(value, step):
        name, bit = step
        size = lax.axis_size(name)
        return value + lax.ppermute(value, name, [(at, at ^ bit) for at in range(size)])

    per_hop = -(-len(steps) // (chips - 1))
    for hop in range(1, chips):
        if hop > 1:
            first_run = scattered(first_sums, first_run, hop)
            second_run = scattered(second_sums, second_run, hop)
        for step in steps[:per_hop]:
            sink_grad = exchange(sink_grad, step)
        steps = steps[per_hop:]
        if hop < chips - 1:
            sink_grad, first_run, second_run = lax.optimization_barrier(
                (sink_grad, first_run, second_run)
            )
    sink_grad = sink_grad[0, :head_count]
    first_total = finished(first_sums, first_run)
    first_back = send(first_others, swap)
    second_back = send(second_others, swap)
    second_total = finished(second_sums, second_run)

    def whole(mine, other):
        return jnp.where(
            core == 0, jnp.concatenate(mine + other, axis=1), jnp.concatenate(other + mine, axis=1)
        )

    wide = width * ratio
    attn_out, query_grad = [
        whole(
            [part[at][:local_rows] for part in (first_out, second_out)],
            [part[:, at * wide : (at + 1) * wide] for part in (first_back, second_back)],
        )
        for at in range(2)
    ]
    key_grad, value_grad = [
        whole(
            *[
                [part[side][:, first : first + width] for part in (first_total, second_total)]
                for side in range(2)
            ]
        )
        for first in (0, width)
    ]
    return (attn_out, query_grad, key_grad, value_grad, sink_grad)


def solution(mesh):
    rows = P(("dp", "ctx"), None)
    return jax.shard_map(
        per_device,
        mesh=mesh,
        in_specs=(rows, rows, rows, rows, P(), P(), P(), P()),
        out_specs=(rows, rows, rows, rows, P()),
        check_vma=False,
    )
```

```python
import functools
import math

import jax
import jax.numpy as jnp
from jax import lax
from jax.experimental import pallas as pl
from jax.experimental.pallas import tpu as pltpu
from jax.sharding import PartitionSpec as P

HD = 128
BLOCK = 128
STREAMS = 2
SCALE = HD**-0.5
LOG2E = math.log2(math.e)
MASKED = -1e30


def fill_table(
    chip, core, group, chips, stretch_len, map_ref, lengths_ref, assign_ref, table_ref
):
    stretches = map_ref.shape[0]
    sequences, documents = lengths_ref.shape
    per_chip = stretches // chips
    per_core = per_chip // 2
    limit = (table_ref.shape[1] - 1) // 2
    sequence = jnp.int32(0)
    for at in range(sequences):
        sequence = jnp.where(group == at, assign_ref[at], sequence)
    ends = []
    total = jnp.int32(0)
    for at in range(documents):
        total = total + lengths_ref[sequence, at] * (BLOCK // stretch_len)
        ends.append(total)

    def first_of_document(stretch):
        first = jnp.int32(0)
        for end in ends:
            first = jnp.where(stretch >= end, end, first)
        return first

    for row in range(per_chip):
        core_of_row = core if row < per_core else 1 - core
        slot = chip * per_chip + core_of_row * per_core + row % per_core
        mine = map_ref[slot]
        first = first_of_document(mine)

        def rows_of(key_slot):
            key_chip = key_slot // per_chip
            inner = key_slot - key_chip * per_chip
            key_core = inner // per_core
            inner = inner - key_core * per_core
            inner = inner + jnp.where(key_core == core, 0, per_core)
            ahead = key_chip - chip
            table = jnp.where(ahead > 0, chips - 2 + ahead, -ahead)
            table = jnp.where(abs(ahead) == chips - 1, 2 * chips - 3, table)
            partial = jnp.where(ahead < 0, ahead + chips, ahead)
            return (
                (table * per_chip + inner) * stretch_len,
                (partial * per_chip + inner) * stretch_len,
            )

        key_row, sum_row = rows_of(slot)
        for at in range(limit):
            table_ref[row, 1 + 2 * at] = key_row
            table_ref[row, 2 + 2 * at] = sum_row

        def visit(key_slot, count):
            other = map_ref[key_slot]
            seen = (other >= first) & (other < mine)

            @pl.when(seen)
            def _():
                key_row, sum_row = rows_of(key_slot)
                table_ref[row, 1 + 2 * count] = key_row
                table_ref[row, 2 + 2 * count] = sum_row

            return count + seen.astype(jnp.int32)

        table_ref[row, 0] = lax.fori_loop(0, stretches, visit, jnp.int32(1))


def attention_kernel(
    shape, map_hbm, lengths_hbm, assign_hbm, sink_hbm, q_hbm, g_hbm, partner_hbm, *refs
):
    heads, ratio, stretch_len, per_chip, chips, limit, stream = shape
    count_in = 2 * chips - 2
    sources, refs = refs[:count_in], refs[count_in:]
    earlier, refs = refs[:stream], refs[stream:]
    o_hbm, dq_hbm, back_hbm, far_hbm = refs[:4]
    partials, refs = refs[4 : 4 + chips], refs[4 + chips :]
    sink_out, kv, q_buf, g_buf, sums, out_buf, part_buf, table_ref, *small, sems = refs
    tiny = (map_hbm, lengths_hbm, assign_hbm, sink_hbm)
    map_ref, lengths_ref, assign_ref, sink_ref = small
    index = lax.axis_index("ctx")
    chip, core = index // 2, index % 2
    rows = per_chip * stretch_len
    local_rows = rows // 2
    wide = heads * ratio * HD
    here = pl.ds(pl.multiple_of((core * STREAMS + stream) * wide, HD), wide)
    last = 4 + count_in
    tables = [
        pltpu.make_async_copy(source, target, sems.at[last + at])
        for at, (source, target) in enumerate(zip(tiny, small))
    ]
    for load in tables:
        load.start()
    loads = [
        (q_hbm.at[:, here], q_buf.at[pl.ds(0, local_rows)]),
        (g_hbm.at[:, here], g_buf.at[pl.ds(0, local_rows)]),
        (
            partner_hbm.at[:, pl.ds(stream * wide, wide)],
            q_buf.at[pl.ds(local_rows, local_rows)],
        ),
        (
            partner_hbm.at[:, pl.ds((STREAMS + stream) * wide, wide)],
            g_buf.at[pl.ds(local_rows, local_rows)],
        ),
    ]
    loads += [(source, kv.at[pl.ds(at * rows, rows)]) for at, source in enumerate(sources)]
    loads = [pltpu.make_async_copy(*pair, sems.at[at]) for at, pair in enumerate(loads)]
    for load in loads:
        load.start()
    for load in tables:
        load.wait()
    fill_table(
        chip,
        core,
        lax.axis_index("dp"),
        chips,
        stretch_len,
        map_ref,
        lengths_ref,
        assign_ref,
        table_ref,
    )
    sums[...] = jnp.zeros_like(sums)
    sink_out[...] = jnp.zeros_like(sink_out)
    block = ratio * stretch_len
    token = lax.broadcasted_iota(jnp.int32, (2 * stretch_len, block), 1) % stretch_len
    place = lax.broadcasted_iota(jnp.int32, (2 * stretch_len, block), 0)
    owner = lax.broadcasted_iota(jnp.int32, (1, block), 1) // stretch_len
    sinks = []
    for head in range(heads):
        first_head = ((core * STREAMS + stream) * heads + head) * ratio
        sink = jnp.zeros((1, block), jnp.float32)
        for at in range(ratio):
            sink = jnp.where(owner == at, sink_ref[first_head + at] * LOG2E, sink)
        sinks.append(sink)
    for load in loads:
        load.wait()

    def take(ref, first, head):
        first_lane = head * ratio * HD
        return jnp.concatenate(
            [
                ref[pl.ds(first, stretch_len), first_lane + at * HD : first_lane + (at + 1) * HD]
                for at in range(ratio)
            ],
            axis=0,
        )

    def put(ref, first, head, value):
        first_lane = head * ratio * HD
        for at in range(ratio):
            ref[pl.ds(first, stretch_len), first_lane + at * HD : first_lane + (at + 1) * HD] = (
                value[at * stretch_len : (at + 1) * stretch_len].astype(ref.dtype)
            )

    def one_block(row, slots):
        count = table_ref[row, 0]
        first = pl.multiple_of(row * stretch_len, stretch_len)
        key_rows = [pl.multiple_of(table_ref[row, 1 + 2 * at], stretch_len) for at in range(slots)]
        sum_rows = [pl.multiple_of(table_ref[row, 2 + 2 * at], stretch_len) for at in range(slots)]
        order = list(range(1, slots - 1)) + [slots - 1, 0]
        empty = jnp.where(count == slots, 0, 4 * stretch_len)
        seen = jnp.where(place < stretch_len, empty, place - stretch_len) <= token
        across = (((1,), (1,)), ((), ()))
        down = (((0,), (0,)), ((), ()))
        lists = [[] for _ in range(6)]
        for head in range(heads):
            query, grad = take(q_buf, first, head), take(g_buf, first, head)
            keys = jnp.concatenate(
                [kv[pl.ds(key_rows[at], stretch_len), head * HD : (head + 1) * HD] for at in order],
                axis=0,
            )
            values = jnp.concatenate(
                [
                    kv[
                        pl.ds(key_rows[at], stretch_len),
                        (heads + head) * HD : (heads + head + 1) * HD,
                    ]
                    for at in order
                ],
                axis=0,
            )
            scores = lax.dot_general(keys, query, across, preferred_element_type=jnp.float32)
            grad_weights = lax.dot_general(values, grad, across, preferred_element_type=jnp.float32)
            for part, value in zip(lists, (query, grad, keys, values, scores, grad_weights)):
                part.append(value)
        mixed = []
        for head in range(heads):
            scores, grad_weights = lists[4][head], lists[5][head]
            edge = jnp.where(seen, scores[(slots - 2) * stretch_len :], MASKED)
            if slots > 2:
                scores = jnp.concatenate([scores[: (slots - 2) * stretch_len], edge], axis=0)
            else:
                scores = edge
            scores = scores * (SCALE * LOG2E)
            row_max = jnp.maximum(sinks[head], jnp.max(scores, axis=0, keepdims=True))
            terms = jnp.exp2(scores - row_max)
            sink_term = jnp.exp2(sinks[head] - row_max)
            inverse = 1.0 / (sink_term + jnp.sum(terms, axis=0, keepdims=True))
            weights = terms * inverse
            row_dot = jnp.sum(weights * grad_weights, axis=0, keepdims=True)
            grad_scores = (weights * (grad_weights - row_dot)).astype(jnp.bfloat16)
            mixed.append((weights.astype(jnp.bfloat16), grad_scores))
            sink_out[head] -= sink_term * inverse * row_dot
        for head in range(heads):
            query, grad, keys, values = (part[head] for part in lists[:4])
            weights_b, grad_scores = mixed[head]
            dv = jnp.dot(weights_b, grad, preferred_element_type=jnp.float32)
            dk = jnp.dot(grad_scores, query, preferred_element_type=jnp.float32)
            attended = lax.dot_general(weights_b, values, down, preferred_element_type=jnp.float32)
            dq = lax.dot_general(grad_scores, keys, down, preferred_element_type=jnp.float32) * SCALE
            put(out_buf, first, head, attended)
            put(out_buf, first, heads + head, dq)
            for spot, at in enumerate(order):
                part = slice(spot * stretch_len, (spot + 1) * stretch_len)
                target = pl.ds(sum_rows[at], stretch_len)
                sums[target, head * HD : (head + 1) * HD] += dk[part]
                sums[target, (heads + head) * HD : (heads + head + 1) * HD] += dv[part]

    widths = []
    width = 2
    while width < limit:
        widths.append(width)
        width += 2
    widths.append(limit)

    def one_row(row, carry):
        count = table_ref[row, 0]
        below = 0
        for width in widths:

            @pl.when((count > below) & (count <= width))
            def _():
                one_block(row, width)

            below = width
        return carry

    lax.fori_loop(0, per_chip, one_row, 0)
    mine, theirs = pl.ds(0, local_rows), pl.ds(local_rows, local_rows)
    stores = [
        (out_buf.at[mine, pl.ds(0, wide)], o_hbm),
        (out_buf.at[mine, pl.ds(wide, wide)], dq_hbm),
        (out_buf.at[theirs], back_hbm),
    ]
    stores = [pltpu.make_async_copy(*pair, sems.at[at]) for at, pair in enumerate(stores)]
    for store in stores:
        store.start()
    if stream:
        vectors = [jnp.concatenate([ref[at] for at in range(heads)], axis=1) for ref in earlier]
        vectors.append(jnp.concatenate([sink_out[at] for at in range(heads)], axis=1))
        slots = part_buf.shape[1] - rows
        slot = lax.broadcasted_iota(jnp.int32, (slots, heads * ratio * stretch_len), 0)
        filled = jnp.zeros(slot.shape, jnp.float32)
        for at, vector in enumerate(vectors):
            for piece in range(3):
                top = vector.astype(jnp.bfloat16).astype(jnp.float32)
                filled = jnp.where(slot == (3 * at + piece) * chips + chip, top, filled)
                vector = vector - top
        filled = filled.astype(jnp.bfloat16)
    far = jnp.where(chip == 0, chips - 1, 1)
    for at in range(chips):
        part = slice(at * rows, (at + 1) * rows)
        part_buf[at, :rows, : heads * HD] = (sums[part, : heads * HD] * SCALE).astype(jnp.bfloat16)
        part_buf[at, :rows, heads * HD :] = sums[part, heads * HD :].astype(jnp.bfloat16)
        if stream:
            part_buf[at, rows:] = filled
        stores.append(pltpu.make_async_copy(part_buf.at[at], partials[at], sems.at[3 + at]))
        stores[-1].start()
    stores.append(pltpu.make_async_copy(part_buf.at[far], far_hbm, sems.at[3 + chips]))
    stores[-1].start()
    for store in stores:
        store.wait()


def attend(
    stream, layout, sinks, queries, out_grad, partner, sources, earlier, chips, limit, ratio
):
    heads = sources[0].shape[1] // (2 * HD)
    rows = sources[0].shape[0]
    per_chip = layout[0].shape[0] // chips
    stretch_len = rows // per_chip
    wide = heads * ratio * HD
    shape = (heads, ratio, stretch_len, per_chip, chips, limit, stream)
    hbm, vmem = pl.BlockSpec(memory_space=pltpu.HBM), pl.BlockSpec(memory_space=pltpu.VMEM)
    sent_rows = rows + (-(-3 * STREAMS * chips // 16) * 16 if stream else 0)
    own = jax.ShapeDtypeStruct((rows // 2, wide), jnp.bfloat16)
    sent = jax.ShapeDtypeStruct((sent_rows, heads * 2 * HD), jnp.bfloat16)
    return pl.pallas_call(
        functools.partial(attention_kernel, shape),
        in_specs=[hbm] * (7 + len(sources)) + [vmem] * len(earlier),
        out_specs=[hbm] * (4 + chips) + [vmem],
        scratch_shapes=[
            pltpu.VMEM((len(sources) * rows, heads * 2 * HD), jnp.bfloat16),
            pltpu.VMEM((rows, wide), jnp.bfloat16),
            pltpu.VMEM((rows, wide), jnp.bfloat16),
            pltpu.VMEM((chips * rows, heads * 2 * HD), jnp.float32),
            pltpu.VMEM((rows, 2 * wide), jnp.bfloat16),
            pltpu.VMEM((chips, sent_rows, heads * 2 * HD), jnp.bfloat16),
            pltpu.SMEM((per_chip, 1 + 2 * limit), jnp.int32),
            *[pltpu.SMEM(part.shape, part.dtype) for part in (*layout, sinks)],
            pltpu.SemaphoreType.DMA((8 + len(sources),)),
        ],
        out_shape=[own, own, jax.ShapeDtypeStruct((rows // 2, 2 * wide), jnp.bfloat16)]
        + [sent] * (1 + chips)
        + [jax.ShapeDtypeStruct((heads, 1, ratio * stretch_len), jnp.float32)],
        compiler_params=pltpu.CompilerParams(vmem_limit_bytes=60 << 20),
        cost_estimate=pl.CostEstimate(
            flops=6 * 2 * heads * rows * ratio * limit * stretch_len * HD,
            transcendentals=heads * rows * ratio * limit * stretch_len,
            bytes_accessed=8 << 20,
        ),
    )(*layout, sinks, queries, out_grad, partner, *sources, *earlier)


def send(value, pairs):
    return lax.ppermute(value, "ctx", pairs)


def along(chips, step, senders):
    return [
        (2 * chip + core, 2 * (chip + step) + core)
        for chip in senders
        if 0 <= chip + step < chips
        for core in range(2)
    ]


def gather_hop(rightward, leftward, hop, chips):
    return (
        send(rightward, along(chips, 1, range(hop - 1, chips))),
        send(leftward, along(chips, -1, range(0, chips - hop + 1))),
    )


def scatter_hop(rightward, leftward, hop, chips):
    return (
        send(rightward, along(chips, 1, range(0, hop))),
        send(leftward, along(chips, -1, range(chips - hop, chips))),
    )


def add(left, right):
    return (left.astype(jnp.float32) + right.astype(jnp.float32)).astype(jnp.bfloat16)


def add3(first, second, third):
    total = first.astype(jnp.float32) + second.astype(jnp.float32) + third.astype(jnp.float32)
    return total.astype(jnp.bfloat16)


def columns(table, first, count):
    return lax.dynamic_slice_in_dim(table, first, count, 1)


def per_device(
    queries, key_input, value_input, out_grad, sink_logits, doc_lengths, assignment, stretch_map
):
    local_rows = queries.shape[0]
    chips = lax.axis_size("ctx") // 2
    stretches = stretch_map.shape[0]
    stretch_len = local_rows * 2 * chips // stretches
    per_chip = stretches // chips
    head_count = sink_logits.shape[0]
    kv_heads = key_input.shape[1] // HD
    ratio = head_count // kv_heads
    limit = stretches // 2
    group = lax.axis_index("dp")
    index = lax.axis_index("ctx")
    chip, core = index // 2, index % 2
    swap = [(2 * at + side, 2 * at + 1 - side) for at in range(chips) for side in range(2)]
    half = kv_heads // 2 * HD
    width = half // STREAMS

    def key_values(side, stream):
        first = side * half + stream * width
        return jnp.concatenate(
            [columns(key_input, first, width), columns(value_input, first, width)], axis=1
        )

    received = send(
        jnp.concatenate([key_values(1 - core, stream) for stream in range(STREAMS)], axis=1), swap
    )
    own = [
        jnp.concatenate(
            [key_values(core, at), received[:, 2 * width * at : 2 * width * (at + 1)]], axis=0
        )
        for at in range(STREAMS)
    ]
    partner = send(
        jnp.concatenate(
            [
                columns(queries, (1 - core) * half * ratio, half * ratio),
                columns(out_grad, (1 - core) * half * ratio, half * ratio),
            ],
            axis=1,
        ),
        swap,
    )
    layout = (stretch_map, doc_lengths, assignment)

    def gathered(stream, hops):
        right, left = hops[-1] if hops else (own[stream], own[stream])
        hop = len(hops) + 1
        if hop < chips - 1:
            return hops + [gather_hop(right, left, hop, chips)]
        ends = along(chips, 1, [chips - 2]) + along(chips, -1, [1])
        return hops + [(send(jnp.where(chip >= chips // 2, right, left), ends),)]

    def compute(stream, hops, earlier):
        right, left = [hop[0] for hop in hops[:-1]], [hop[1] for hop in hops[:-1]]
        results = attend(
            stream, layout, sink_logits, queries, out_grad, partner,
            [own[stream]] + right + left + list(hops[-1]), earlier, chips, limit, ratio,
        )
        return results[:3], results[3], results[4:-1], results[-1]

    def scattered(far, partials, running, hop):
        if hop == 1:
            ends = along(chips, 1, [0]) + along(chips, -1, [chips - 1])
            return (send(far, ends),) * 2
        return scatter_hop(
            add(partials[chips - hop], running[0]), add(partials[hop], running[1]), hop, chips
        )

    def finished(partials, running):
        total = add3(partials[0], *running)
        return total, send(total[local_rows:], swap)

    first_hops, second_hops = [], []
    for _ in range(1, chips):
        first_hops = gathered(0, first_hops)
        second_hops = gathered(1, second_hops)
    first_out, first_far, first_sums, first_sink = compute(0, first_hops, [])
    first_run = scattered(first_far, None, None, 1)
    second_out, second_far, second_sums, _ = compute(1, second_hops, [first_sink])
    second_run = scattered(second_far, None, None, 1)
    for hop in range(2, chips):
        second_run = scattered(None, second_sums, second_run, hop)
        first_run = scattered(None, first_sums, first_run, hop)
    second_total = finished(second_sums, second_run)
    first_total = finished(first_sums, first_run)
    first_back, second_back = send(first_out[2], swap), send(second_out[2], swap)

    def sink_sums(slots):
        slots = slots.astype(jnp.float32)[: 3 * STREAMS * chips]
        slots = jnp.sum(slots.reshape(STREAMS, 3 * chips, -1), axis=1)
        return jnp.sum(slots.reshape(head_count // 2, -1), axis=1)

    mine, theirs = sink_sums(second_total[0][2 * local_rows :]), sink_sums(
        second_total[1][local_rows:]
    )
    sink_grad = jnp.where(core == 0, jnp.concatenate([mine, theirs]), jnp.concatenate([theirs, mine]))
    size = lax.axis_size("dp")
    slot = lax.broadcasted_iota(jnp.int32, (max(size, 8), 128), 0)
    sink_grad = jnp.pad(sink_grad.reshape(1, -1), ((0, 0), (0, 128 - head_count)))
    sink_grad = jnp.where(slot == lax.axis_index("dp"), sink_grad, 0.0)
    others = [
        lax.ppermute(sink_grad, "dp", [(at, at ^ bit) for at in range(size)])
        for bit in range(1, size)
    ]
    sink_grad = jnp.sum(functools.reduce(jnp.add, others, sink_grad), axis=0)[:head_count]

    def whole(mine, other):
        return jnp.where(
            core == 0, jnp.concatenate(mine + other, axis=1), jnp.concatenate(other + mine, axis=1)
        )

    wide = width * ratio
    attn_out, query_grad = [
        whole(
            [part[at] for part in (first_out, second_out)],
            [part[:, at * wide : (at + 1) * wide] for part in (first_back, second_back)],
        )
        for at in range(2)
    ]
    key_grad, value_grad = [
        whole(
            *[
                [part[side][:local_rows, at : at + width] for part in (first_total, second_total)]
                for side in range(2)
            ]
        )
        for at in (0, width)
    ]
    return (attn_out, query_grad, key_grad, value_grad, sink_grad)


def solution(mesh):
    rows = P(("dp", "ctx"), None)
    return jax.shard_map(
        per_device,
        mesh=mesh,
        in_specs=(rows, rows, rows, rows, P(), P(), P(), P()),
        out_specs=(rows, rows, rows, rows, P()),
        check_vma=False,
    )
```

```python
import functools
import math

import jax
import jax.numpy as jnp
from jax import lax
from jax.experimental import pallas as pl
from jax.experimental.pallas import tpu as pltpu
from jax.sharding import PartitionSpec as P

HD = 128
BLOCK = 128
STREAMS = 2
SCALE = HD**-0.5
LOG2E = math.log2(math.e)
MASKED = -1e30


def fill_table(
    chip, core, group, chips, stretch_len, map_ref, lengths_ref, assign_ref, table_ref
):
    stretches = map_ref.shape[0]
    sequences, documents = lengths_ref.shape
    per_chip = stretches // chips
    per_core = per_chip // 2
    limit = (table_ref.shape[1] - 1) // 2
    sequence = jnp.int32(0)
    for at in range(sequences):
        sequence = jnp.where(group == at, assign_ref[at], sequence)
    ends = []
    total = jnp.int32(0)
    for at in range(documents):
        total = total + lengths_ref[sequence, at] * (BLOCK // stretch_len)
        ends.append(total)

    def first_of_document(stretch):
        first = jnp.int32(0)
        for end in ends:
            first = jnp.where(stretch >= end, end, first)
        return first

    def rows_of(key_slot):
        key_chip, inner = key_slot // per_chip, key_slot % per_chip
        inner = inner % per_core + jnp.where(inner // per_core == core, 0, per_core)
        ahead = key_chip - chip
        table = jnp.where(ahead > 0, chips - 2 + ahead, -ahead)
        table = jnp.where(abs(ahead) == chips - 1, 2 * chips - 3, table)
        partial = jnp.where(ahead < 0, ahead + chips, ahead)
        return (table * per_chip + inner) * stretch_len, (partial * per_chip + inner) * stretch_len

    own, firsts, counts, own_rows = [], [], [], []
    for row in range(per_chip):
        own.append(map_ref[chip * per_chip + (core if row < per_core else 1 - core) * per_core + row % per_core])
        firsts.append(first_of_document(own[row]))
        own_rows.append((row * stretch_len, row * stretch_len))
        table_ref[row, 1], table_ref[row, 2] = own_rows[row]
        counts.append(jnp.int32(1))
    for key_slot in range(stretches):
        other = map_ref[key_slot]
        key_row, sum_row = rows_of(key_slot)
        for row in range(per_chip):
            table_ref[row, 1 + 2 * counts[row]] = key_row
            table_ref[row, 2 + 2 * counts[row]] = sum_row
            seen = (other >= firsts[row]) & (other < own[row])
            counts[row] = counts[row] + seen.astype(jnp.int32)
    for row in range(per_chip):
        table_ref[row, 1 + 2 * counts[row]], table_ref[row, 2 + 2 * counts[row]] = own_rows[row]
        table_ref[row, 0] = counts[row]


def attention_kernel(shape, sink_hbm, q_hbm, g_hbm, partner_hbm, *refs):
    heads, ratio, stretch_len, per_chip, chips, limit, stream = shape
    count_in = 2 * chips - 2
    sources, refs = refs[:count_in], refs[count_in:]
    layout, refs = (refs[:1], refs[1:]) if stream else (refs[:3], refs[3:])
    earlier, refs = refs[:stream], refs[stream:]
    o_hbm, dq_hbm, back_hbm, far_hbm = refs[:4]
    partials, refs = refs[4 : 4 + chips], refs[4 + chips :]
    if stream:
        sink_out, *refs = refs
    else:
        sink_out, table_ref, *refs = refs
    kv, q_buf, g_buf, sums, out_buf, part_buf, *small, sink_ref, sems = refs
    if stream:
        (table_ref,) = small
    index = lax.axis_index("ctx")
    chip, core = index // 2, index % 2
    rows = per_chip * stretch_len
    local_rows = rows // 2
    wide = heads * ratio * HD
    here = pl.ds(pl.multiple_of((core * STREAMS + stream) * wide, HD), wide)
    last = 4 + count_in
    tables = [
        pltpu.make_async_copy(source, target, sems.at[last + at])
        for at, (source, target) in enumerate(zip((*layout, sink_hbm), (*small, sink_ref)))
    ]
    for load in tables:
        load.start()
    loads = [
        (q_hbm.at[:, here], q_buf.at[pl.ds(0, local_rows)]),
        (g_hbm.at[:, here], g_buf.at[pl.ds(0, local_rows)]),
        (
            partner_hbm.at[:, pl.ds(stream * wide, wide)],
            q_buf.at[pl.ds(local_rows, local_rows)],
        ),
        (
            partner_hbm.at[:, pl.ds((STREAMS + stream) * wide, wide)],
            g_buf.at[pl.ds(local_rows, local_rows)],
        ),
    ]
    held = [chip >= 0] * 5
    held += [chip >= hop for hop in range(1, chips - 1)]
    held += [chip < chips - hop for hop in range(1, chips - 1)]
    held.append((chip == 0) | (chip == chips - 1))
    loads += [(source, kv.at[pl.ds(at * rows, rows)]) for at, source in enumerate(sources)]
    loads = [pltpu.make_async_copy(*pair, sems.at[at]) for at, pair in enumerate(loads)]
    for at, load in enumerate(loads):
        if at < 5:
            load.start()
        else:
            pl.when(held[at])(load.start)
    for load in tables:
        load.wait()
    if not stream:
        fill_table(
            chip, core, lax.axis_index("dp"), chips, stretch_len, *small, table_ref
        )
    sums[...] = jnp.zeros_like(sums)
    sink_out[...] = jnp.zeros_like(sink_out)
    block = ratio * stretch_len
    token = lax.broadcasted_iota(jnp.int32, (2 * stretch_len, block), 1) % stretch_len
    place = lax.broadcasted_iota(jnp.int32, (2 * stretch_len, block), 0)
    owner = lax.broadcasted_iota(jnp.int32, (1, block), 1) // stretch_len
    sinks = []
    for head in range(heads):
        first_head = ((core * STREAMS + stream) * heads + head) * ratio
        sink = jnp.zeros((1, block), jnp.float32)
        for at in range(ratio):
            sink = jnp.where(owner == at, sink_ref[first_head + at] * LOG2E, sink)
        sinks.append(sink)
    for at, load in enumerate(loads):
        if at < 5:
            load.wait()
        else:
            pl.when(held[at])(load.wait)

    def take(ref, first, head):
        first_lane = head * ratio * HD
        return jnp.concatenate(
            [
                ref[pl.ds(first, stretch_len), first_lane + at * HD : first_lane + (at + 1) * HD]
                for at in range(ratio)
            ],
            axis=0,
        )

    def put(ref, first, head, value):
        first_lane = head * ratio * HD
        for at in range(ratio):
            ref[pl.ds(first, stretch_len), first_lane + at * HD : first_lane + (at + 1) * HD] = (
                value[at * stretch_len : (at + 1) * stretch_len].astype(ref.dtype)
            )

    def one_block(row, slots):
        count = table_ref[row, 0]
        first = pl.multiple_of(row * stretch_len, stretch_len)
        key_rows = [pl.multiple_of(table_ref[row, 1 + 2 * at], stretch_len) for at in range(slots)]
        sum_rows = [pl.multiple_of(table_ref[row, 2 + 2 * at], stretch_len) for at in range(slots)]
        order = list(range(1, slots - 1)) + [slots - 1, 0]
        empty = jnp.where(count == slots, 0, 4 * stretch_len)
        seen = jnp.where(place < stretch_len, empty, place - stretch_len) <= token
        across = (((1,), (1,)), ((), ()))
        down = (((0,), (0,)), ((), ()))
        lists = [[] for _ in range(6)]
        for head in range(heads):
            query, grad = take(q_buf, first, head), take(g_buf, first, head)
            keys = jnp.concatenate(
                [kv[pl.ds(key_rows[at], stretch_len), head * HD : (head + 1) * HD] for at in order],
                axis=0,
            )
            values = jnp.concatenate(
                [
                    kv[
                        pl.ds(key_rows[at], stretch_len),
                        (heads + head) * HD : (heads + head + 1) * HD,
                    ]
                    for at in order
                ],
                axis=0,
            )
            scores = lax.dot_general(keys, query, across, preferred_element_type=jnp.float32)
            grad_weights = lax.dot_general(values, grad, across, preferred_element_type=jnp.float32)
            for part, value in zip(lists, (query, grad, keys, values, scores, grad_weights)):
                part.append(value)
        mixed = []
        for head in range(heads):
            scores, grad_weights = lists[4][head], lists[5][head]
            edge = jnp.where(seen, scores[(slots - 2) * stretch_len :], MASKED)
            if slots > 2:
                scores = jnp.concatenate([scores[: (slots - 2) * stretch_len], edge], axis=0)
            else:
                scores = edge
            scores = scores * (SCALE * LOG2E)
            row_max = jnp.maximum(sinks[head], jnp.max(scores, axis=0, keepdims=True))
            terms = jnp.exp2(scores - row_max)
            sink_term = jnp.exp2(sinks[head] - row_max)
            inverse = 1.0 / (sink_term + jnp.sum(terms, axis=0, keepdims=True))
            weights = terms * inverse
            row_dot = jnp.sum(weights * grad_weights, axis=0, keepdims=True)
            grad_scores = (weights * (grad_weights - row_dot)).astype(jnp.bfloat16)
            mixed.append((weights.astype(jnp.bfloat16), grad_scores))
            sink_out[head] -= sink_term * inverse * row_dot
        for head in range(heads):
            query, grad, keys, values = (part[head] for part in lists[:4])
            weights_b, grad_scores = mixed[head]
            dv = jnp.dot(weights_b, grad, preferred_element_type=jnp.float32)
            dk = jnp.dot(grad_scores, query, preferred_element_type=jnp.float32)
            attended = lax.dot_general(weights_b, values, down, preferred_element_type=jnp.float32)
            dq = lax.dot_general(grad_scores, keys, down, preferred_element_type=jnp.float32) * SCALE
            put(out_buf, first, head, attended)
            put(out_buf, first, heads + head, dq)
            for spot, at in enumerate(order):
                part = slice(spot * stretch_len, (spot + 1) * stretch_len)
                target = pl.ds(sum_rows[at], stretch_len)
                sums[target, head * HD : (head + 1) * HD] += dk[part]
                sums[target, (heads + head) * HD : (heads + head + 1) * HD] += dv[part]

    widths = []
    width = 2
    while width < limit:
        widths.append(width)
        width += 2
    widths.append(limit)

    def one_row(row, carry):
        count = table_ref[row, 0]
        below = 0
        for width in widths:

            @pl.when((count > below) & (count <= width))
            def _():
                one_block(row, width)

            below = width
        return carry

    lax.fori_loop(0, per_chip, one_row, 0)
    mine, theirs = pl.ds(0, local_rows), pl.ds(local_rows, local_rows)
    stores = [
        (out_buf.at[mine, pl.ds(0, wide)], o_hbm),
        (out_buf.at[mine, pl.ds(wide, wide)], dq_hbm),
        (out_buf.at[theirs], back_hbm),
    ]
    stores = [pltpu.make_async_copy(*pair, sems.at[at]) for at, pair in enumerate(stores)]
    for store in stores:
        store.start()
    if stream:
        vectors = [jnp.concatenate([ref[at] for at in range(heads)], axis=1) for ref in earlier]
        vectors.append(jnp.concatenate([sink_out[at] for at in range(heads)], axis=1))
        slots = part_buf.shape[1] - rows
        slot = lax.broadcasted_iota(jnp.int32, (slots, heads * ratio * stretch_len), 0)
        filled = jnp.zeros(slot.shape, jnp.float32)
        for at, vector in enumerate(vectors):
            for piece in range(3):
                top = vector.astype(jnp.bfloat16).astype(jnp.float32)
                filled = jnp.where(slot == (3 * at + piece) * chips + chip, top, filled)
                vector = vector - top
        filled = filled.astype(jnp.bfloat16)
    far = jnp.where(chip == 0, chips - 1, 1)
    for at in range(chips):
        part = slice(at * rows, (at + 1) * rows)
        part_buf[at, :rows, : heads * HD] = (sums[part, : heads * HD] * SCALE).astype(jnp.bfloat16)
        part_buf[at, :rows, heads * HD :] = sums[part, heads * HD :].astype(jnp.bfloat16)
        if stream:
            part_buf[at, rows:] = filled
        stores.append(pltpu.make_async_copy(part_buf.at[at], partials[at], sems.at[3 + at]))
        stores[-1].start()
    stores.append(pltpu.make_async_copy(part_buf.at[far], far_hbm, sems.at[3 + chips]))
    stores[-1].start()
    for store in stores:
        store.wait()


def attend(
    stream, layout, sinks, queries, out_grad, partner, sources, earlier, chips, limit, ratio
):
    heads = sources[0].shape[1] // (2 * HD)
    rows = sources[0].shape[0]
    per_chip = layout[0].shape[0] // (1 if stream else chips)
    stretch_len = rows // per_chip
    wide = heads * ratio * HD
    shape = (heads, ratio, stretch_len, per_chip, chips, limit, stream)
    smem, hbm = pl.BlockSpec(memory_space=pltpu.SMEM), pl.BlockSpec(memory_space=pltpu.HBM)
    vmem = pl.BlockSpec(memory_space=pltpu.VMEM)
    sent_rows = rows + (-(-3 * STREAMS * chips // 16) * 16 if stream else 0)
    own = jax.ShapeDtypeStruct((rows // 2, wide), jnp.bfloat16)
    sent = jax.ShapeDtypeStruct((sent_rows, heads * 2 * HD), jnp.bfloat16)
    return pl.pallas_call(
        functools.partial(attention_kernel, shape),
        in_specs=[hbm] * (4 + len(sources) + len(layout)) + [vmem] * len(earlier),
        out_specs=[hbm] * (4 + chips) + [vmem] + ([] if stream else [smem]),
        scratch_shapes=[
            pltpu.VMEM((len(sources) * rows, heads * 2 * HD), jnp.bfloat16),
            pltpu.VMEM((rows, wide), jnp.bfloat16),
            pltpu.VMEM((rows, wide), jnp.bfloat16),
            pltpu.VMEM((chips * rows, heads * 2 * HD), jnp.float32),
            pltpu.VMEM((rows, 2 * wide), jnp.bfloat16),
            pltpu.VMEM((chips, sent_rows, heads * 2 * HD), jnp.bfloat16),
            *[pltpu.SMEM(part.shape, part.dtype) for part in layout],
            pltpu.SMEM(sinks.shape, sinks.dtype),
            pltpu.SemaphoreType.DMA((8 + len(sources),)),
        ],
        out_shape=[own, own, jax.ShapeDtypeStruct((rows // 2, 2 * wide), jnp.bfloat16)]
        + [sent] * (1 + chips)
        + [jax.ShapeDtypeStruct((heads, 1, ratio * stretch_len), jnp.float32)]
        + ([] if stream else [jax.ShapeDtypeStruct((per_chip, 3 + 2 * limit), jnp.int32)]),
        compiler_params=pltpu.CompilerParams(vmem_limit_bytes=60 << 20),
        cost_estimate=pl.CostEstimate(
            flops=6 * 2 * heads * rows * ratio * limit * stretch_len * HD,
            transcendentals=heads * rows * ratio * limit * stretch_len,
            bytes_accessed=8 << 20,
        ),
    )(sinks, queries, out_grad, partner, *sources, *layout, *earlier)


def send(value, pairs):
    return lax.ppermute(value, "ctx", pairs)


def along(chips, step, senders):
    return [
        (2 * chip + core, 2 * (chip + step) + core)
        for chip in senders
        if 0 <= chip + step < chips
        for core in range(2)
    ]


def gather_hop(rightward, leftward, hop, chips):
    return (
        send(rightward, along(chips, 1, range(hop - 1, chips))),
        send(leftward, along(chips, -1, range(0, chips - hop + 1))),
    )


def scatter_hop(rightward, leftward, hop, chips):
    return (
        send(rightward, along(chips, 1, range(0, hop))),
        send(leftward, along(chips, -1, range(chips - hop, chips))),
    )


def add(left, right):
    return (left.astype(jnp.float32) + right.astype(jnp.float32)).astype(jnp.bfloat16)


def add3(first, second, third):
    total = first.astype(jnp.float32) + second.astype(jnp.float32) + third.astype(jnp.float32)
    return total.astype(jnp.bfloat16)


def columns(table, first, count):
    return lax.dynamic_slice_in_dim(table, first, count, 1)


def per_device(
    queries, key_input, value_input, out_grad, sink_logits, doc_lengths, assignment, stretch_map
):
    local_rows = queries.shape[0]
    chips = lax.axis_size("ctx") // 2
    stretches = stretch_map.shape[0]
    stretch_len = local_rows * 2 * chips // stretches
    per_chip = stretches // chips
    head_count = sink_logits.shape[0]
    kv_heads = key_input.shape[1] // HD
    ratio = head_count // kv_heads
    limit = stretches // 2
    group = lax.axis_index("dp")
    index = lax.axis_index("ctx")
    chip, core = index // 2, index % 2
    swap = [(2 * at + side, 2 * at + 1 - side) for at in range(chips) for side in range(2)]
    half = kv_heads // 2 * HD
    width = half // STREAMS

    def key_values(side, stream):
        first = side * half + stream * width
        return jnp.concatenate(
            [columns(key_input, first, width), columns(value_input, first, width)], axis=1
        )

    received = send(
        jnp.concatenate([key_values(1 - core, stream) for stream in range(STREAMS)], axis=1), swap
    )
    own = [
        jnp.concatenate(
            [key_values(core, at), received[:, 2 * width * at : 2 * width * (at + 1)]], axis=0
        )
        for at in range(STREAMS)
    ]
    partner = send(
        jnp.concatenate(
            [
                columns(queries, (1 - core) * half * ratio, half * ratio),
                columns(out_grad, (1 - core) * half * ratio, half * ratio),
            ],
            axis=1,
        ),
        swap,
    )
    def gathered(stream, hops):
        right, left = hops[-1] if hops else (own[stream], own[stream])
        hop = len(hops) + 1
        if hop < chips - 1:
            return hops + [gather_hop(right, left, hop, chips)]
        ends = along(chips, 1, [chips - 2]) + along(chips, -1, [1])
        return hops + [(send(jnp.where(chip >= chips // 2, right, left), ends),)]

    def compute(stream, layout, hops, earlier):
        right, left = [hop[0] for hop in hops[:-1]], [hop[1] for hop in hops[:-1]]
        results = attend(
            stream, layout, sink_logits, queries, out_grad, partner,
            [own[stream]] + right + left + list(hops[-1]), earlier, chips, limit, ratio,
        )
        return results[:3], results[3], results[4 : 4 + chips], results[4 + chips :]

    def added(partials, running, hop):
        return add(partials[chips - hop], running[0]), add(partials[hop], running[1])

    def scattered(far, partials, running, hop):
        if hop == 1:
            ends = along(chips, 1, [0]) + along(chips, -1, [chips - 1])
            return (send(far, ends),) * 2
        return scatter_hop(*added(partials, running, hop), hop, chips)

    def finished(partials, running):
        total = add3(partials[0], *running)
        return total, send(total[local_rows:], swap)

    first_hops, second_hops = [], []
    for hop in range(1, chips):
        first_hops = gathered(0, first_hops)
        second_hops = gathered(1, second_hops)
        if hop == chips - 2:
            partner, first_hops[-1] = lax.optimization_barrier((partner, first_hops[-1]))
    layout = (stretch_map, doc_lengths, assignment)
    first_out, first_far, first_sums, (first_sink, table) = compute(0, layout, first_hops, [])
    first_run = scattered(first_far, None, None, 1)
    second_out, second_far, second_sums, _ = compute(1, (table,), second_hops, [first_sink])
    second_run = scattered(second_far, None, None, 1)
    both = send(jnp.concatenate([first_out[2], second_out[2]], axis=1), swap)
    first_back, second_back = both[:, : both.shape[1] // 2], both[:, both.shape[1] // 2 :]
    for hop in range(2, chips):
        second_run = scattered(None, second_sums, second_run, hop)
        first_run = scattered(None, first_sums, first_run, hop)
    def whole(mine, other):
        return jnp.where(
            core == 0, jnp.concatenate(mine + other, axis=1), jnp.concatenate(other + mine, axis=1)
        )

    wide = width * ratio
    attn_out, query_grad = [
        whole(
            [part[at] for part in (first_out, second_out)],
            [part[:, at * wide : (at + 1) * wide] for part in (first_back, second_back)],
        )
        for at in range(2)
    ]
    (attn_out, query_grad), first_run, second_run = lax.optimization_barrier(
        ((attn_out, query_grad), first_run, second_run)
    )
    second_total = finished(second_sums, second_run)
    first_total = finished(first_sums, first_run)

    def sink_sums(slots):
        slots = slots.astype(jnp.float32)[: 3 * STREAMS * chips]
        slots = jnp.sum(slots.reshape(STREAMS, 3 * chips, -1), axis=1)
        return jnp.sum(slots.reshape(head_count // 2, -1), axis=1)

    mine, theirs = sink_sums(second_total[0][2 * local_rows :]), sink_sums(
        second_total[1][local_rows:]
    )
    sink_grad = jnp.where(core == 0, jnp.concatenate([mine, theirs]), jnp.concatenate([theirs, mine]))
    size = lax.axis_size("dp")
    slot = lax.broadcasted_iota(jnp.int32, (max(size, 8), 128), 0)
    sink_grad = jnp.pad(sink_grad.reshape(1, -1), ((0, 0), (0, 128 - head_count)))
    sink_grad = jnp.where(slot == lax.axis_index("dp"), sink_grad, 0.0)
    others = [
        lax.ppermute(sink_grad, "dp", [(at, at ^ bit) for at in range(size)])
        for bit in range(1, size)
    ]
    sink_grad = jnp.sum(functools.reduce(jnp.add, others, sink_grad), axis=0)[:head_count]

    key_grad, value_grad = [
        whole(
            *[
                [part[side][:local_rows, at : at + width] for part in (first_total, second_total)]
                for side in range(2)
            ]
        )
        for at in (0, width)
    ]
    return (attn_out, query_grad, key_grad, value_grad, sink_grad)


def solution(mesh):
    rows = P(("dp", "ctx"), None)
    return jax.shard_map(
        per_device,
        mesh=mesh,
        in_specs=(rows, rows, rows, rows, P(), P(), P(), P()),
        out_specs=(rows, rows, rows, rows, P()),
        check_vma=False,
    )
```

```python
import functools
import math

import jax
import jax.numpy as jnp
from jax import lax
from jax.experimental import pallas as pl
from jax.experimental.pallas import tpu as pltpu
from jax.sharding import PartitionSpec as P

HD = 128
BLOCK = 128
STREAMS = 2
SCALE = HD**-0.5
LOG2E = math.log2(math.e)
MASKED = -1e30


def fill_table(
    chip, core, group, chips, stretch_len, map_ref, lengths_ref, assign_ref, table_ref
):
    stretches = map_ref.shape[0]
    sequences, documents = lengths_ref.shape
    per_chip = stretches // chips
    per_core = per_chip // 2
    limit = (table_ref.shape[1] - 1) // 2
    sequence = jnp.int32(0)
    for at in range(sequences):
        sequence = jnp.where(group == at, assign_ref[at], sequence)
    ends = []
    total = jnp.int32(0)
    for at in range(documents):
        total = total + lengths_ref[sequence, at] * (BLOCK // stretch_len)
        ends.append(total)

    def first_of_document(stretch):
        first = jnp.int32(0)
        for end in ends:
            first = jnp.where(stretch >= end, end, first)
        return first

    def rows_of(key_slot):
        key_chip, inner = key_slot // per_chip, key_slot % per_chip
        inner = inner % per_core + jnp.where(inner // per_core == core, 0, per_core)
        ahead = key_chip - chip
        table = jnp.where(ahead > 0, chips - 2 + ahead, -ahead)
        table = jnp.where(abs(ahead) == chips - 1, 2 * chips - 3, table)
        partial = jnp.where(ahead < 0, ahead + chips, ahead)
        return (table * per_chip + inner) * stretch_len, (partial * per_chip + inner) * stretch_len

    own, firsts, counts, own_rows = [], [], [], []
    for row in range(per_chip):
        own.append(map_ref[chip * per_chip + (core if row < per_core else 1 - core) * per_core + row % per_core])
        firsts.append(first_of_document(own[row]))
        own_rows.append((row * stretch_len, row * stretch_len))
        table_ref[row, 1], table_ref[row, 2] = own_rows[row]
        counts.append(jnp.int32(1))
    for key_slot in range(stretches):
        other = map_ref[key_slot]
        key_row, sum_row = rows_of(key_slot)
        for row in range(per_chip):
            table_ref[row, 1 + 2 * counts[row]] = key_row
            table_ref[row, 2 + 2 * counts[row]] = sum_row
            seen = (other >= firsts[row]) & (other < own[row])
            counts[row] = counts[row] + seen.astype(jnp.int32)
    for row in range(per_chip):
        table_ref[row, 1 + 2 * counts[row]], table_ref[row, 2 + 2 * counts[row]] = own_rows[row]
        table_ref[row, 0] = counts[row]


def attention_kernel(shape, sink_hbm, q_hbm, g_hbm, partner_hbm, *refs):
    heads, ratio, stretch_len, per_chip, chips, limit, stream = shape
    count_in = 2 * chips - 2
    sources, refs = refs[:count_in], refs[count_in:]
    layout, refs = (refs[:1], refs[1:]) if stream else (refs[:3], refs[3:])
    earlier, refs = refs[:stream], refs[stream:]
    o_hbm, dq_hbm, back_hbm, far_hbm = refs[:4]
    partials, refs = refs[4 : 4 + chips], refs[4 + chips :]
    if stream:
        sink_out, *refs = refs
    else:
        sink_out, table_ref, *refs = refs
    kv, q_buf, g_buf, sums, out_buf, part_buf, *small, sink_ref, sems = refs
    if stream:
        (table_ref,) = small
    index = lax.axis_index("ctx")
    chip, core = index // 2, index % 2
    rows = per_chip * stretch_len
    local_rows = rows // 2
    wide = heads * ratio * HD
    here = pl.ds(pl.multiple_of((core * STREAMS + stream) * wide, HD), wide)
    last = 4 + count_in
    tables = [
        pltpu.make_async_copy(source, target, sems.at[last + at])
        for at, (source, target) in enumerate(zip((*layout, sink_hbm), (*small, sink_ref)))
    ]
    for load in tables:
        load.start()
    loads = [
        (q_hbm.at[:, here], q_buf.at[pl.ds(0, local_rows)]),
        (g_hbm.at[:, here], g_buf.at[pl.ds(0, local_rows)]),
        (
            partner_hbm.at[:, pl.ds(stream * wide, wide)],
            q_buf.at[pl.ds(local_rows, local_rows)],
        ),
        (
            partner_hbm.at[:, pl.ds((STREAMS + stream) * wide, wide)],
            g_buf.at[pl.ds(local_rows, local_rows)],
        ),
    ]
    held = [chip >= 0] * 5
    held += [chip >= hop for hop in range(1, chips - 1)]
    held += [chip < chips - hop for hop in range(1, chips - 1)]
    held.append((chip == 0) | (chip == chips - 1))
    loads += [(source, kv.at[pl.ds(at * rows, rows)]) for at, source in enumerate(sources)]
    loads = [pltpu.make_async_copy(*pair, sems.at[at]) for at, pair in enumerate(loads)]
    for at, load in enumerate(loads):
        if at < 5:
            load.start()
        else:
            pl.when(held[at])(load.start)
    for load in tables:
        load.wait()
    if not stream:
        fill_table(
            chip, core, lax.axis_index("dp"), chips, stretch_len, *small, table_ref
        )
    sums[...] = jnp.zeros_like(sums)
    sink_out[...] = jnp.zeros_like(sink_out)
    block = ratio * stretch_len
    token = lax.broadcasted_iota(jnp.int32, (2 * stretch_len, block), 1) % stretch_len
    place = lax.broadcasted_iota(jnp.int32, (2 * stretch_len, block), 0)
    owner = lax.broadcasted_iota(jnp.int32, (1, block), 1) // stretch_len
    sinks = []
    for head in range(heads):
        first_head = ((core * STREAMS + stream) * heads + head) * ratio
        sink = jnp.zeros((1, block), jnp.float32)
        for at in range(ratio):
            sink = jnp.where(owner == at, sink_ref[first_head + at] * LOG2E, sink)
        sinks.append(sink)
    for at, load in enumerate(loads):
        if at < 5:
            load.wait()
        else:
            pl.when(held[at])(load.wait)

    def take(ref, first, head):
        first_lane = head * ratio * HD
        return jnp.concatenate(
            [
                ref[pl.ds(first, stretch_len), first_lane + at * HD : first_lane + (at + 1) * HD]
                for at in range(ratio)
            ],
            axis=0,
        )

    def put(ref, first, head, value):
        first_lane = head * ratio * HD
        for at in range(ratio):
            ref[pl.ds(first, stretch_len), first_lane + at * HD : first_lane + (at + 1) * HD] = (
                value[at * stretch_len : (at + 1) * stretch_len].astype(ref.dtype)
            )

    def one_block(row, slots):
        count = table_ref[row, 0]
        first = pl.multiple_of(row * stretch_len, stretch_len)
        key_rows = [pl.multiple_of(table_ref[row, 1 + 2 * at], stretch_len) for at in range(slots)]
        sum_rows = [pl.multiple_of(table_ref[row, 2 + 2 * at], stretch_len) for at in range(slots)]
        order = list(range(1, slots - 1)) + [slots - 1, 0]
        empty = jnp.where(count == slots, 0, 4 * stretch_len)
        seen = jnp.where(place < stretch_len, empty, place - stretch_len) <= token
        across = (((1,), (1,)), ((), ()))
        down = (((0,), (0,)), ((), ()))
        lists = [[] for _ in range(6)]
        for head in range(heads):
            query, grad = take(q_buf, first, head), take(g_buf, first, head)
            keys = jnp.concatenate(
                [kv[pl.ds(key_rows[at], stretch_len), head * HD : (head + 1) * HD] for at in order],
                axis=0,
            )
            values = jnp.concatenate(
                [
                    kv[
                        pl.ds(key_rows[at], stretch_len),
                        (heads + head) * HD : (heads + head + 1) * HD,
                    ]
                    for at in order
                ],
                axis=0,
            )
            scores = lax.dot_general(keys, query, across, preferred_element_type=jnp.float32)
            grad_weights = lax.dot_general(values, grad, across, preferred_element_type=jnp.float32)
            for part, value in zip(lists, (query, grad, keys, values, scores, grad_weights)):
                part.append(value)
        mixed = []
        for head in range(heads):
            scores, grad_weights = lists[4][head], lists[5][head]
            edge = jnp.where(seen, scores[(slots - 2) * stretch_len :], MASKED)
            if slots > 2:
                scores = jnp.concatenate([scores[: (slots - 2) * stretch_len], edge], axis=0)
            else:
                scores = edge
            scores = scores * (SCALE * LOG2E)
            row_max = jnp.maximum(sinks[head], jnp.max(scores, axis=0, keepdims=True))
            terms = jnp.exp2(scores - row_max)
            sink_term = jnp.exp2(sinks[head] - row_max)
            inverse = 1.0 / (sink_term + jnp.sum(terms, axis=0, keepdims=True))
            weights = terms * inverse
            row_dot = jnp.sum(weights * grad_weights, axis=0, keepdims=True)
            grad_scores = (weights * (grad_weights - row_dot)).astype(jnp.bfloat16)
            mixed.append((weights.astype(jnp.bfloat16), grad_scores))
            sink_out[head] -= sink_term * inverse * row_dot
        for head in range(heads):
            query, grad, keys, values = (part[head] for part in lists[:4])
            weights_b, grad_scores = mixed[head]
            dv = jnp.dot(weights_b, grad, preferred_element_type=jnp.float32)
            dk = jnp.dot(grad_scores, query, preferred_element_type=jnp.float32)
            attended = lax.dot_general(weights_b, values, down, preferred_element_type=jnp.float32)
            dq = lax.dot_general(grad_scores, keys, down, preferred_element_type=jnp.float32) * SCALE
            put(out_buf, first, head, attended)
            put(out_buf, first, heads + head, dq)
            for spot, at in enumerate(order):
                part = slice(spot * stretch_len, (spot + 1) * stretch_len)
                target = pl.ds(sum_rows[at], stretch_len)
                sums[target, head * HD : (head + 1) * HD] += dk[part]
                sums[target, (heads + head) * HD : (heads + head + 1) * HD] += dv[part]

    widths = []
    width = 2
    while width < limit:
        widths.append(width)
        width += 2
    widths.append(limit)

    def one_row(row, carry):
        count = table_ref[row, 0]
        below = 0
        for width in widths:

            @pl.when((count > below) & (count <= width))
            def _():
                one_block(row, width)

            below = width
        return carry

    lax.fori_loop(0, per_chip, one_row, 0)
    mine, theirs = pl.ds(0, local_rows), pl.ds(local_rows, local_rows)
    stores = [
        (out_buf.at[mine, pl.ds(0, wide)], o_hbm),
        (out_buf.at[mine, pl.ds(wide, wide)], dq_hbm),
        (out_buf.at[theirs], back_hbm),
    ]
    stores = [pltpu.make_async_copy(*pair, sems.at[at]) for at, pair in enumerate(stores)]
    for store in stores:
        store.start()
    if stream:
        vectors = [jnp.concatenate([ref[at] for at in range(heads)], axis=1) for ref in earlier]
        vectors.append(jnp.concatenate([sink_out[at] for at in range(heads)], axis=1))
        slots = part_buf.shape[1] - rows
        slot = lax.broadcasted_iota(jnp.int32, (slots, heads * ratio * stretch_len), 0)
        filled = jnp.zeros(slot.shape, jnp.float32)
        for at, vector in enumerate(vectors):
            for piece in range(3):
                top = vector.astype(jnp.bfloat16).astype(jnp.float32)
                filled = jnp.where(slot == (3 * at + piece) * chips + chip, top, filled)
                vector = vector - top
        filled = filled.astype(jnp.bfloat16)
    far = jnp.where(chip == 0, chips - 1, 1)
    for at in range(chips):
        part = slice(at * rows, (at + 1) * rows)
        part_buf[at, :rows, : heads * HD] = (sums[part, : heads * HD] * SCALE).astype(jnp.bfloat16)
        part_buf[at, :rows, heads * HD :] = sums[part, heads * HD :].astype(jnp.bfloat16)
        if stream:
            part_buf[at, rows:] = filled
        stores.append(pltpu.make_async_copy(part_buf.at[at], partials[at], sems.at[3 + at]))
        stores[-1].start()
    stores.append(pltpu.make_async_copy(part_buf.at[far], far_hbm, sems.at[3 + chips]))
    stores[-1].start()
    for store in stores:
        store.wait()


def attend(
    stream, layout, sinks, queries, out_grad, partner, sources, earlier, chips, limit, ratio
):
    heads = sources[0].shape[1] // (2 * HD)
    rows = sources[0].shape[0]
    per_chip = layout[0].shape[0] // (1 if stream else chips)
    stretch_len = rows // per_chip
    wide = heads * ratio * HD
    shape = (heads, ratio, stretch_len, per_chip, chips, limit, stream)
    smem, hbm = pl.BlockSpec(memory_space=pltpu.SMEM), pl.BlockSpec(memory_space=pltpu.HBM)
    vmem = pl.BlockSpec(memory_space=pltpu.VMEM)
    sent_rows = rows + (-(-3 * STREAMS * chips // 16) * 16 if stream else 0)
    own = jax.ShapeDtypeStruct((rows // 2, wide), jnp.bfloat16)
    sent = jax.ShapeDtypeStruct((sent_rows, heads * 2 * HD), jnp.bfloat16)
    return pl.pallas_call(
        functools.partial(attention_kernel, shape),
        in_specs=[hbm] * (4 + len(sources) + len(layout)) + [vmem] * len(earlier),
        out_specs=[hbm] * (4 + chips) + [vmem] + ([] if stream else [smem]),
        scratch_shapes=[
            pltpu.VMEM((len(sources) * rows, heads * 2 * HD), jnp.bfloat16),
            pltpu.VMEM((rows, wide), jnp.bfloat16),
            pltpu.VMEM((rows, wide), jnp.bfloat16),
            pltpu.VMEM((chips * rows, heads * 2 * HD), jnp.float32),
            pltpu.VMEM((rows, 2 * wide), jnp.bfloat16),
            pltpu.VMEM((chips, sent_rows, heads * 2 * HD), jnp.bfloat16),
            *[pltpu.SMEM(part.shape, part.dtype) for part in layout],
            pltpu.SMEM(sinks.shape, sinks.dtype),
            pltpu.SemaphoreType.DMA((8 + len(sources),)),
        ],
        out_shape=[own, own, jax.ShapeDtypeStruct((rows // 2, 2 * wide), jnp.bfloat16)]
        + [sent] * (1 + chips)
        + [jax.ShapeDtypeStruct((heads, 1, ratio * stretch_len), jnp.float32)]
        + ([] if stream else [jax.ShapeDtypeStruct((per_chip, 3 + 2 * limit), jnp.int32)]),
        compiler_params=pltpu.CompilerParams(vmem_limit_bytes=60 << 20),
        cost_estimate=pl.CostEstimate(
            flops=0 if stream else 6 * 2 * heads * rows * ratio * limit * stretch_len * HD,
            transcendentals=0,
            bytes_accessed=1024 if stream else 8 << 20,
        ),
    )(sinks, queries, out_grad, partner, *sources, *layout, *earlier)


def send(value, pairs):
    return lax.ppermute(value, "ctx", pairs)


def along(chips, step, senders):
    return [
        (2 * chip + core, 2 * (chip + step) + core)
        for chip in senders
        if 0 <= chip + step < chips
        for core in range(2)
    ]


def gather_hop(rightward, leftward, hop, chips):
    return (
        send(rightward, along(chips, 1, range(hop - 1, chips))),
        send(leftward, along(chips, -1, range(0, chips - hop + 1))),
    )


def scatter_hop(rightward, leftward, hop, chips):
    return (
        send(rightward, along(chips, 1, range(0, hop))),
        send(leftward, along(chips, -1, range(chips - hop, chips))),
    )


def add(left, right):
    return (left.astype(jnp.float32) + right.astype(jnp.float32)).astype(jnp.bfloat16)


def add3(first, second, third):
    total = first.astype(jnp.float32) + second.astype(jnp.float32) + third.astype(jnp.float32)
    return total.astype(jnp.bfloat16)


def columns(table, first, count):
    return lax.dynamic_slice_in_dim(table, first, count, 1)


def per_device(
    queries, key_input, value_input, out_grad, sink_logits, doc_lengths, assignment, stretch_map
):
    local_rows = queries.shape[0]
    chips = lax.axis_size("ctx") // 2
    stretches = stretch_map.shape[0]
    stretch_len = local_rows * 2 * chips // stretches
    per_chip = stretches // chips
    head_count = sink_logits.shape[0]
    kv_heads = key_input.shape[1] // HD
    ratio = head_count // kv_heads
    limit = stretches // 2
    group = lax.axis_index("dp")
    index = lax.axis_index("ctx")
    chip, core = index // 2, index % 2
    swap = [(2 * at + side, 2 * at + 1 - side) for at in range(chips) for side in range(2)]
    half = kv_heads // 2 * HD
    width = half // STREAMS

    def key_values(side, stream):
        first = side * half + stream * width
        return jnp.concatenate(
            [columns(key_input, first, width), columns(value_input, first, width)], axis=1
        )

    received = send(
        jnp.concatenate([key_values(1 - core, stream) for stream in range(STREAMS)], axis=1), swap
    )
    own = [
        jnp.concatenate(
            [key_values(core, at), received[:, 2 * width * at : 2 * width * (at + 1)]], axis=0
        )
        for at in range(STREAMS)
    ]
    partner = send(
        jnp.concatenate(
            [
                columns(queries, (1 - core) * half * ratio, half * ratio),
                columns(out_grad, (1 - core) * half * ratio, half * ratio),
            ],
            axis=1,
        ),
        swap,
    )
    def gathered(stream, hops):
        right, left = hops[-1] if hops else (own[stream], own[stream])
        hop = len(hops) + 1
        if hop < chips - 1:
            return hops + [gather_hop(right, left, hop, chips)]
        ends = along(chips, 1, [chips - 2]) + along(chips, -1, [1])
        return hops + [(send(jnp.where(chip >= chips // 2, right, left), ends),)]

    def compute(stream, layout, hops, earlier):
        right, left = [hop[0] for hop in hops[:-1]], [hop[1] for hop in hops[:-1]]
        results = attend(
            stream, layout, sink_logits, queries, out_grad, partner,
            [own[stream]] + right + left + list(hops[-1]), earlier, chips, limit, ratio,
        )
        return results[:3], results[3], results[4 : 4 + chips], results[4 + chips :]

    def added(partials, running, hop):
        return add(partials[chips - hop], running[0]), add(partials[hop], running[1])

    def scattered(far, partials, running, hop):
        if hop == 1:
            ends = along(chips, 1, [0]) + along(chips, -1, [chips - 1])
            return (send(far, ends),) * 2
        return scatter_hop(*added(partials, running, hop), hop, chips)

    def finished(partials, running):
        total = add3(partials[0], *running)
        return total, send(total[local_rows:], swap)

    first_hops, second_hops = [], []
    for hop in range(1, chips):
        first_hops = gathered(0, first_hops)
        second_hops = gathered(1, second_hops)
        if hop == chips - 2:
            partner, first_hops[-1] = lax.optimization_barrier((partner, first_hops[-1]))
    layout = (stretch_map, doc_lengths, assignment)
    first_out, first_far, first_sums, (first_sink, table) = compute(0, layout, first_hops, [])
    first_run = scattered(first_far, None, None, 1)
    second_out, second_far, second_sums, _ = compute(1, (table,), second_hops, [first_sink])
    second_run = scattered(second_far, None, None, 1)
    both = send(jnp.concatenate([first_out[2], second_out[2]], axis=1), swap)
    first_back, second_back = both[:, : both.shape[1] // 2], both[:, both.shape[1] // 2 :]
    for hop in range(2, chips):
        second_run = scattered(None, second_sums, second_run, hop)
        first_run = scattered(None, first_sums, first_run, hop)
    def whole(mine, other):
        return jnp.where(
            core == 0, jnp.concatenate(mine + other, axis=1), jnp.concatenate(other + mine, axis=1)
        )

    wide = width * ratio
    attn_out, query_grad = [
        whole(
            [part[at] for part in (first_out, second_out)],
            [part[:, at * wide : (at + 1) * wide] for part in (first_back, second_back)],
        )
        for at in range(2)
    ]
    (attn_out, query_grad), first_run, second_run = lax.optimization_barrier(
        ((attn_out, query_grad), first_run, second_run)
    )
    second_total = finished(second_sums, second_run)
    first_total = finished(first_sums, first_run)

    def sink_sums(slots):
        slots = slots.astype(jnp.float32)[: 3 * STREAMS * chips]
        slots = jnp.sum(slots.reshape(STREAMS, 3 * chips, -1), axis=1)
        return jnp.sum(slots.reshape(head_count // 2, -1), axis=1)

    mine, theirs = sink_sums(second_total[0][2 * local_rows :]), sink_sums(
        second_total[1][local_rows:]
    )
    sink_grad = jnp.where(core == 0, jnp.concatenate([mine, theirs]), jnp.concatenate([theirs, mine]))
    size = lax.axis_size("dp")
    slot = lax.broadcasted_iota(jnp.int32, (max(size, 8), 128), 0)
    sink_grad = jnp.pad(sink_grad.reshape(1, -1), ((0, 0), (0, 128 - head_count)))
    sink_grad = jnp.where(slot == lax.axis_index("dp"), sink_grad, 0.0)
    others = [
        lax.ppermute(sink_grad, "dp", [(at, at ^ bit) for at in range(size)])
        for bit in range(1, size)
    ]
    sink_grad = jnp.sum(functools.reduce(jnp.add, others, sink_grad), axis=0)[:head_count]

    key_grad, value_grad = [
        whole(
            *[
                [part[side][:local_rows, at : at + width] for part in (first_total, second_total)]
                for side in range(2)
            ]
        )
        for at in (0, width)
    ]
    return (attn_out, query_grad, key_grad, value_grad, sink_grad)


def solution(mesh):
    rows = P(("dp", "ctx"), None)
    return jax.shard_map(
        per_device,
        mesh=mesh,
        in_specs=(rows, rows, rows, rows, P(), P(), P(), P()),
        out_specs=(rows, rows, rows, rows, P()),
        check_vma=False,
    )
```

```python
import functools
import math

import jax
import jax.numpy as jnp
from jax import lax
from jax.experimental import pallas as pl
from jax.experimental.pallas import tpu as pltpu
from jax.sharding import PartitionSpec as P

HD = 128
BLOCK = 128
STREAMS = 2
SCALE = HD**-0.5
LOG2E = math.log2(math.e)
MASKED = -1e30


def fill_table(
    chip, core, group, chips, stretch_len, map_ref, lengths_ref, assign_ref, table_ref
):
    stretches = map_ref.shape[0]
    sequences, documents = lengths_ref.shape
    per_chip = stretches // chips
    per_core = per_chip // 2
    limit = (table_ref.shape[1] - 1) // 2
    sequence = jnp.int32(0)
    for at in range(sequences):
        sequence = jnp.where(group == at, assign_ref[at], sequence)
    ends = []
    total = jnp.int32(0)
    for at in range(documents):
        total = total + lengths_ref[sequence, at] * (BLOCK // stretch_len)
        ends.append(total)

    def first_of_document(stretch):
        first = jnp.int32(0)
        for end in ends:
            first = jnp.where(stretch >= end, end, first)
        return first

    def rows_of(key_slot):
        key_chip, inner = key_slot // per_chip, key_slot % per_chip
        inner = inner % per_core + jnp.where(inner // per_core == core, 0, per_core)
        ahead = key_chip - chip
        table = jnp.where(ahead > 0, chips - 2 + ahead, -ahead)
        table = jnp.where(abs(ahead) == chips - 1, 2 * chips - 3, table)
        partial = jnp.where(ahead < 0, ahead + chips, ahead)
        return (table * per_chip + inner) * stretch_len, (partial * per_chip + inner) * stretch_len

    own, firsts, counts, own_rows = [], [], [], []
    for row in range(per_chip):
        own.append(map_ref[chip * per_chip + (core if row < per_core else 1 - core) * per_core + row % per_core])
        firsts.append(first_of_document(own[row]))
        own_rows.append((row * stretch_len, row * stretch_len))
        table_ref[row, 1], table_ref[row, 2] = own_rows[row]
        counts.append(jnp.int32(1))
    for key_slot in range(stretches):
        other = map_ref[key_slot]
        key_row, sum_row = rows_of(key_slot)
        for row in range(per_chip):
            table_ref[row, 1 + 2 * counts[row]] = key_row
            table_ref[row, 2 + 2 * counts[row]] = sum_row
            seen = (other >= firsts[row]) & (other < own[row])
            counts[row] = counts[row] + seen.astype(jnp.int32)
    for row in range(per_chip):
        table_ref[row, 1 + 2 * counts[row]], table_ref[row, 2 + 2 * counts[row]] = own_rows[row]
        table_ref[row, 0] = counts[row]


def attention_kernel(shape, sink_hbm, q_hbm, g_hbm, partner_hbm, *refs):
    heads, ratio, stretch_len, per_chip, chips, limit, stream = shape
    count_in = 2 * chips - 2
    sources, refs = refs[:count_in], refs[count_in:]
    layout, refs = (refs[:1], refs[1:]) if stream else (refs[:3], refs[3:])
    earlier, refs = refs[:stream], refs[stream:]
    o_hbm, dq_hbm, back_hbm, far_hbm = refs[:4]
    partials, refs = refs[4 : 4 + chips], refs[4 + chips :]
    if stream:
        sink_out, *refs = refs
    else:
        sink_out, table_ref, *refs = refs
    kv, q_buf, g_buf, sums, out_buf, part_buf, *small, sink_ref, sems = refs
    if stream:
        (table_ref,) = small
    index = lax.axis_index("ctx")
    chip, core = index // 2, index % 2
    rows = per_chip * stretch_len
    local_rows = rows // 2
    wide = heads * ratio * HD
    here = pl.ds(pl.multiple_of((core * STREAMS + stream) * wide, HD), wide)
    last = 4 + count_in
    tables = [
        pltpu.make_async_copy(source, target, sems.at[last + at])
        for at, (source, target) in enumerate(zip((*layout, sink_hbm), (*small, sink_ref)))
    ]
    for load in tables:
        load.start()
    loads = [
        (q_hbm.at[:, here], q_buf.at[pl.ds(0, local_rows)]),
        (g_hbm.at[:, here], g_buf.at[pl.ds(0, local_rows)]),
        (
            partner_hbm.at[:, pl.ds(stream * wide, wide)],
            q_buf.at[pl.ds(local_rows, local_rows)],
        ),
        (
            partner_hbm.at[:, pl.ds((STREAMS + stream) * wide, wide)],
            g_buf.at[pl.ds(local_rows, local_rows)],
        ),
    ]
    held = [chip >= 0] * 5
    held += [chip >= hop for hop in range(1, chips - 1)]
    held += [chip < chips - hop for hop in range(1, chips - 1)]
    held.append((chip == 0) | (chip == chips - 1))
    loads += [(source, kv.at[pl.ds(at * rows, rows)]) for at, source in enumerate(sources)]
    loads = [pltpu.make_async_copy(*pair, sems.at[at]) for at, pair in enumerate(loads)]
    for at, load in enumerate(loads):
        if at < 5:
            load.start()
        else:
            pl.when(held[at])(load.start)
    for load in tables:
        load.wait()
    if not stream:
        fill_table(
            chip, core, lax.axis_index("dp"), chips, stretch_len, *small, table_ref
        )
    sums[...] = jnp.zeros_like(sums)
    sink_out[...] = jnp.zeros_like(sink_out)
    block = ratio * stretch_len
    token = lax.broadcasted_iota(jnp.int32, (2 * stretch_len, block), 1) % stretch_len
    place = lax.broadcasted_iota(jnp.int32, (2 * stretch_len, block), 0)
    owner = lax.broadcasted_iota(jnp.int32, (1, block), 1) // stretch_len
    sinks = []
    for head in range(heads):
        first_head = ((core * STREAMS + stream) * heads + head) * ratio
        sink = jnp.zeros((1, block), jnp.float32)
        for at in range(ratio):
            sink = jnp.where(owner == at, sink_ref[first_head + at] * LOG2E, sink)
        sinks.append(sink)
    for at, load in enumerate(loads):
        if at < 5:
            load.wait()
        else:
            pl.when(held[at])(load.wait)

    def take(ref, first, head):
        first_lane = head * ratio * HD
        return jnp.concatenate(
            [
                ref[pl.ds(first, stretch_len), first_lane + at * HD : first_lane + (at + 1) * HD]
                for at in range(ratio)
            ],
            axis=0,
        )

    def put(ref, first, head, value):
        first_lane = head * ratio * HD
        for at in range(ratio):
            ref[pl.ds(first, stretch_len), first_lane + at * HD : first_lane + (at + 1) * HD] = (
                value[at * stretch_len : (at + 1) * stretch_len].astype(ref.dtype)
            )

    def one_block(row, slots):
        count = table_ref[row, 0]
        first = pl.multiple_of(row * stretch_len, stretch_len)
        key_rows = [pl.multiple_of(table_ref[row, 1 + 2 * at], stretch_len) for at in range(slots)]
        sum_rows = [pl.multiple_of(table_ref[row, 2 + 2 * at], stretch_len) for at in range(slots)]
        order = list(range(1, slots - 1)) + [slots - 1, 0]
        empty = jnp.where(count == slots, 0, 4 * stretch_len)
        seen = jnp.where(place < stretch_len, empty, place - stretch_len) <= token
        across = (((1,), (1,)), ((), ()))
        down = (((0,), (0,)), ((), ()))
        lists = [[] for _ in range(6)]
        for head in range(heads):
            query, grad = take(q_buf, first, head), take(g_buf, first, head)
            keys = jnp.concatenate(
                [kv[pl.ds(key_rows[at], stretch_len), head * HD : (head + 1) * HD] for at in order],
                axis=0,
            )
            values = jnp.concatenate(
                [
                    kv[
                        pl.ds(key_rows[at], stretch_len),
                        (heads + head) * HD : (heads + head + 1) * HD,
                    ]
                    for at in order
                ],
                axis=0,
            )
            scores = lax.dot_general(keys, query, across, preferred_element_type=jnp.float32)
            grad_weights = lax.dot_general(values, grad, across, preferred_element_type=jnp.float32)
            for part, value in zip(lists, (query, grad, keys, values, scores, grad_weights)):
                part.append(value)
        mixed = []
        for head in range(heads):
            scores, grad_weights = lists[4][head], lists[5][head]
            edge = jnp.where(seen, scores[(slots - 2) * stretch_len :], MASKED)
            if slots > 2:
                scores = jnp.concatenate([scores[: (slots - 2) * stretch_len], edge], axis=0)
            else:
                scores = edge
            scores = scores * (SCALE * LOG2E)
            row_max = jnp.maximum(sinks[head], jnp.max(scores, axis=0, keepdims=True))
            terms = jnp.exp2(scores - row_max)
            sink_term = jnp.exp2(sinks[head] - row_max)
            inverse = 1.0 / (sink_term + jnp.sum(terms, axis=0, keepdims=True))
            weights = terms * inverse
            row_dot = jnp.sum(weights * grad_weights, axis=0, keepdims=True)
            grad_scores = (weights * (grad_weights - row_dot)).astype(jnp.bfloat16)
            mixed.append((weights.astype(jnp.bfloat16), grad_scores))
            sink_out[head] -= sink_term * inverse * row_dot
        for head in range(heads):
            query, grad, keys, values = (part[head] for part in lists[:4])
            weights_b, grad_scores = mixed[head]
            dv = jnp.dot(weights_b, grad, preferred_element_type=jnp.float32)
            dk = jnp.dot(grad_scores, query, preferred_element_type=jnp.float32)
            attended = lax.dot_general(weights_b, values, down, preferred_element_type=jnp.float32)
            dq = lax.dot_general(grad_scores, keys, down, preferred_element_type=jnp.float32) * SCALE
            put(out_buf, first, head, attended)
            put(out_buf, first, heads + head, dq)
            for spot, at in enumerate(order):
                part = slice(spot * stretch_len, (spot + 1) * stretch_len)
                target = pl.ds(sum_rows[at], stretch_len)
                sums[target, head * HD : (head + 1) * HD] += dk[part]
                sums[target, (heads + head) * HD : (heads + head + 1) * HD] += dv[part]

    widths = []
    width = 2
    while width < limit:
        widths.append(width)
        width += 2
    widths.append(limit)

    def one_row(row, carry):
        count = table_ref[row, 0]
        below = 0
        for width in widths:

            @pl.when((count > below) & (count <= width))
            def _():
                one_block(row, width)

            below = width
        return carry

    lax.fori_loop(0, per_chip, one_row, 0)
    mine, theirs = pl.ds(0, local_rows), pl.ds(local_rows, local_rows)
    stores = [
        (out_buf.at[mine, pl.ds(0, wide)], o_hbm),
        (out_buf.at[mine, pl.ds(wide, wide)], dq_hbm),
        (out_buf.at[theirs], back_hbm),
    ]
    stores = [pltpu.make_async_copy(*pair, sems.at[at]) for at, pair in enumerate(stores)]
    for store in stores:
        store.start()
    if stream:
        vectors = [jnp.concatenate([ref[at] for at in range(heads)], axis=1) for ref in earlier]
        vectors.append(jnp.concatenate([sink_out[at] for at in range(heads)], axis=1))
        slots = part_buf.shape[1] - rows
        slot = lax.broadcasted_iota(jnp.int32, (slots, heads * ratio * stretch_len), 0)
        filled = jnp.zeros(slot.shape, jnp.float32)
        for at, vector in enumerate(vectors):
            for piece in range(3):
                top = vector.astype(jnp.bfloat16).astype(jnp.float32)
                filled = jnp.where(slot == (3 * at + piece) * chips + chip, top, filled)
                vector = vector - top
        filled = filled.astype(jnp.bfloat16)
    far = jnp.where(chip == 0, chips - 1, 1)
    for at in range(chips):
        part = slice(at * rows, (at + 1) * rows)
        part_buf[at, :rows, : heads * HD] = (sums[part, : heads * HD] * SCALE).astype(jnp.bfloat16)
        part_buf[at, :rows, heads * HD :] = sums[part, heads * HD :].astype(jnp.bfloat16)
        if stream:
            part_buf[at, rows:] = filled
        stores.append(pltpu.make_async_copy(part_buf.at[at], partials[at], sems.at[3 + at]))
        stores[-1].start()
    stores.append(pltpu.make_async_copy(part_buf.at[far], far_hbm, sems.at[3 + chips]))
    stores[-1].start()
    for store in stores:
        store.wait()


def attend(
    stream, layout, sinks, queries, out_grad, partner, sources, earlier, chips, limit, ratio
):
    heads = sources[0].shape[1] // (2 * HD)
    rows = sources[0].shape[0]
    per_chip = layout[0].shape[0] // (1 if stream else chips)
    stretch_len = rows // per_chip
    wide = heads * ratio * HD
    shape = (heads, ratio, stretch_len, per_chip, chips, limit, stream)
    smem, hbm = pl.BlockSpec(memory_space=pltpu.SMEM), pl.BlockSpec(memory_space=pltpu.HBM)
    vmem = pl.BlockSpec(memory_space=pltpu.VMEM)
    sent_rows = rows + (-(-3 * STREAMS * chips // 16) * 16 if stream else 0)
    own = jax.ShapeDtypeStruct((rows // 2, wide), jnp.bfloat16)
    sent = jax.ShapeDtypeStruct((sent_rows, heads * 2 * HD), jnp.bfloat16)
    return pl.pallas_call(
        functools.partial(attention_kernel, shape),
        in_specs=[hbm] * (4 + len(sources) + len(layout)) + [vmem] * len(earlier),
        out_specs=[hbm] * (4 + chips) + [vmem] + ([] if stream else [smem]),
        scratch_shapes=[
            pltpu.VMEM((len(sources) * rows, heads * 2 * HD), jnp.bfloat16),
            pltpu.VMEM((rows, wide), jnp.bfloat16),
            pltpu.VMEM((rows, wide), jnp.bfloat16),
            pltpu.VMEM((chips * rows, heads * 2 * HD), jnp.float32),
            pltpu.VMEM((rows, 2 * wide), jnp.bfloat16),
            pltpu.VMEM((chips, sent_rows, heads * 2 * HD), jnp.bfloat16),
            *[pltpu.SMEM(part.shape, part.dtype) for part in layout],
            pltpu.SMEM(sinks.shape, sinks.dtype),
            pltpu.SemaphoreType.DMA((8 + len(sources),)),
        ],
        out_shape=[own, own, jax.ShapeDtypeStruct((rows // 2, 2 * wide), jnp.bfloat16)]
        + [sent] * (1 + chips)
        + [jax.ShapeDtypeStruct((heads, 1, ratio * stretch_len), jnp.float32)]
        + ([] if stream else [jax.ShapeDtypeStruct((per_chip, 3 + 2 * limit), jnp.int32)]),
        compiler_params=pltpu.CompilerParams(vmem_limit_bytes=60 << 20),
        cost_estimate=pl.CostEstimate(
            flops=0 if stream else 6 * 2 * heads * rows * ratio * limit * stretch_len * HD,
            transcendentals=0,
            bytes_accessed=1024 if stream else 8 << 20,
        ),
    )(sinks, queries, out_grad, partner, *sources, *layout, *earlier)


def send(value, pairs):
    return lax.ppermute(value, "ctx", pairs)


def along(chips, step, senders):
    return [
        (2 * chip + core, 2 * (chip + step) + core)
        for chip in senders
        if 0 <= chip + step < chips
        for core in range(2)
    ]


def gather_hop(rightward, leftward, hop, chips):
    return (
        send(rightward, along(chips, 1, range(hop - 1, chips))),
        send(leftward, along(chips, -1, range(0, chips - hop + 1))),
    )


def scatter_hop(rightward, leftward, hop, chips):
    return (
        send(rightward, along(chips, 1, range(0, hop))),
        send(leftward, along(chips, -1, range(chips - hop, chips))),
    )


def add(left, right):
    return (left.astype(jnp.float32) + right.astype(jnp.float32)).astype(jnp.bfloat16)


def add3(first, second, third):
    total = first.astype(jnp.float32) + second.astype(jnp.float32) + third.astype(jnp.float32)
    return total.astype(jnp.bfloat16)


def columns(table, first, count):
    return lax.dynamic_slice_in_dim(table, first, count, 1)


def per_device(
    queries, key_input, value_input, out_grad, sink_logits, doc_lengths, assignment, stretch_map
):
    local_rows = queries.shape[0]
    chips = lax.axis_size("ctx") // 2
    stretches = stretch_map.shape[0]
    stretch_len = local_rows * 2 * chips // stretches
    per_chip = stretches // chips
    head_count = sink_logits.shape[0]
    kv_heads = key_input.shape[1] // HD
    ratio = head_count // kv_heads
    limit = stretches // 2
    group = lax.axis_index("dp")
    index = lax.axis_index("ctx")
    chip, core = index // 2, index % 2
    swap = [(2 * at + side, 2 * at + 1 - side) for at in range(chips) for side in range(2)]
    half = kv_heads // 2 * HD
    width = half // STREAMS

    def key_values(side, stream):
        first = side * half + stream * width
        return jnp.concatenate(
            [columns(key_input, first, width), columns(value_input, first, width)], axis=1
        )

    received = send(
        jnp.concatenate([key_values(1 - core, stream) for stream in range(STREAMS)], axis=1), swap
    )
    own = [
        jnp.concatenate(
            [key_values(core, at), received[:, 2 * width * at : 2 * width * (at + 1)]], axis=0
        )
        for at in range(STREAMS)
    ]
    partner = send(
        jnp.concatenate(
            [
                columns(queries, (1 - core) * half * ratio, half * ratio),
                columns(out_grad, (1 - core) * half * ratio, half * ratio),
            ],
            axis=1,
        ),
        swap,
    )
    def gathered(stream, hops):
        right, left = hops[-1] if hops else (own[stream], own[stream])
        hop = len(hops) + 1
        if hop < chips - 1:
            return hops + [gather_hop(right, left, hop, chips)]
        ends = along(chips, 1, [chips - 2]) + along(chips, -1, [1])
        return hops + [(send(jnp.where(chip >= chips // 2, right, left), ends),)]

    def compute(stream, layout, hops, earlier):
        right, left = [hop[0] for hop in hops[:-1]], [hop[1] for hop in hops[:-1]]
        results = attend(
            stream, layout, sink_logits, queries, out_grad, partner,
            [own[stream]] + right + left + list(hops[-1]), earlier, chips, limit, ratio,
        )
        return results[:3], results[3], results[4 : 4 + chips], results[4 + chips :]

    def added(partials, running, hop):
        return add(partials[chips - hop], running[0]), add(partials[hop], running[1])

    def scattered(far, partials, running, hop):
        if hop == 1:
            ends = along(chips, 1, [0]) + along(chips, -1, [chips - 1])
            return (send(far, ends),) * 2
        return scatter_hop(*added(partials, running, hop), hop, chips)

    first_hops, second_hops = [], []
    for hop in range(1, chips):
        first_hops = gathered(0, first_hops)
        second_hops = gathered(1, second_hops)
        if hop == chips - 2:
            partner, first_hops[-1] = lax.optimization_barrier((partner, first_hops[-1]))
    layout = (stretch_map, doc_lengths, assignment)
    first_out, first_far, first_sums, (first_sink, table) = compute(0, layout, first_hops, [])
    first_run = scattered(first_far, None, None, 1)
    second_out, second_far, second_sums, _ = compute(1, (table,), second_hops, [first_sink])
    second_run = scattered(second_far, None, None, 1)
    both = send(jnp.concatenate([first_out[2], second_out[2]], axis=1), swap)
    first_back, second_back = both[:, : both.shape[1] // 2], both[:, both.shape[1] // 2 :]
    for hop in range(2, chips):
        second_run = scattered(None, second_sums, second_run, hop)
        first_run = scattered(None, first_sums, first_run, hop)
    def whole(mine, other):
        return jnp.where(
            core == 0, jnp.concatenate(mine + other, axis=1), jnp.concatenate(other + mine, axis=1)
        )

    wide = width * ratio
    attn_out, query_grad = [
        whole(
            [part[at] for part in (first_out, second_out)],
            [part[:, at * wide : (at + 1) * wide] for part in (first_back, second_back)],
        )
        for at in range(2)
    ]
    (attn_out, query_grad), first_run, second_run = lax.optimization_barrier(
        ((attn_out, query_grad), first_run, second_run)
    )
    second_sum = add3(second_sums[0], *second_run)
    first_sum = add3(first_sums[0], *first_run)
    theirs = send(
        jnp.concatenate([second_sum[local_rows:], first_sum[local_rows:]], axis=0), swap
    )
    count = second_sum.shape[0] - local_rows
    second_total, first_total = (second_sum, theirs[:count]), (first_sum, theirs[count:])

    def sink_sums(slots):
        slots = slots.astype(jnp.float32)[: 3 * STREAMS * chips]
        slots = jnp.sum(slots.reshape(STREAMS, 3 * chips, -1), axis=1)
        return jnp.sum(slots.reshape(head_count // 2, -1), axis=1)

    mine, theirs = sink_sums(second_total[0][2 * local_rows :]), sink_sums(
        second_total[1][local_rows:]
    )
    sink_grad = jnp.where(core == 0, jnp.concatenate([mine, theirs]), jnp.concatenate([theirs, mine]))
    size = lax.axis_size("dp")
    slot = lax.broadcasted_iota(jnp.int32, (max(size, 8), 128), 0)
    sink_grad = jnp.pad(sink_grad.reshape(1, -1), ((0, 0), (0, 128 - head_count)))
    sink_grad = jnp.where(slot == lax.axis_index("dp"), sink_grad, 0.0)
    others = [
        lax.ppermute(sink_grad, "dp", [(at, at ^ bit) for at in range(size)])
        for bit in range(1, size)
    ]
    sink_grad = jnp.sum(functools.reduce(jnp.add, others, sink_grad), axis=0)[:head_count]

    key_grad, value_grad = [
        whole(
            *[
                [part[side][:local_rows, at : at + width] for part in (first_total, second_total)]
                for side in range(2)
            ]
        )
        for at in (0, width)
    ]
    return (attn_out, query_grad, key_grad, value_grad, sink_grad)


def solution(mesh):
    rows = P(("dp", "ctx"), None)
    return jax.shard_map(
        per_device,
        mesh=mesh,
        in_specs=(rows, rows, rows, rows, P(), P(), P(), P()),
        out_specs=(rows, rows, rows, rows, P()),
        check_vma=False,
    )
```
